512 devices in a mesh: rows: 64 (over z_lo, y, core), ang: 8 (over z_hi, x).
Axes of the slice: x: 4, y: 4, z: 16 (z_hi: 2, z_lo: 8; z = z_hi * 8 + z_lo), core: 2. Of those that a mesh axis runs over, the one named last changes fastest.
Arguments:
- measured: bfloat16 [8, 2048, 2, 2048], P('ang', 'rows'), may hold values from -6 to 6
- slices: bfloat16 [2, 2048, 2, 2048], P(None, 'rows', None, 'ang'), may hold values from -5 to 5
- kernel_taps: bfloat16 [2, 65], replicated, may hold values from -1.25 to 1.25
- angle_freq: float32 [128, 2], replicated, may hold values from -40 to 40
- chosen: int32 [8], P('ang'), may hold values from 0 to 127
Outputs:
- grad_near: float32 [2048, 2, 2048], P('rows', None, 'ang')
- grad_far: float32 [2048, 2, 2048], P('rows', None, 'ang')
The draws below stay inside these ranges and needn't reach their ends.
Inputs may be any that keep to these rules, and one draw needn't show every extreme that they name: `chosen`: indices into the angle table; an index may repeat.
All inputs are finite; a program needn't handle non-finite values.
Results may differ from the reference program's by a relative error of at most 0.014.
Values may be sent and summed in bfloat16 or wider, within the bound.
A program may use at most 64 MiB of HBM per device.

```python
import math
import jax
import jax.numpy as jnp

N = 2048
TAPS = 65
ANGLES_ALL = 128
ANGLES = 8


def set_ends(values, own_key, smallest, high):
    dims = values.shape
    place = [jax.random.randint(jax.random.fold_in(own_key, axis), (), 0, dims[axis]) for axis in range(len(dims))]
    values = values.at[tuple(place)].set(smallest)
    longest = dims.index(max(dims))
    place[longest] = (place[longest] + 1) % dims[longest]
    return values.at[tuple(place)].set(high)


def level_of(stream_key, extent, split, least, top_value):
    def one(axis_at, blocks):
        steps = jax.random.uniform(jax.random.fold_in(jax.random.fold_in(stream_key, 6), axis_at), (blocks,), jnp.float32, least / len(split), top_value / len(split))
        return jnp.repeat(jnp.exp(steps), extent[axis_at] // blocks).reshape((-1,) + (1,) * (len(extent) - axis_at - 1))

    factor_of = one(*split[0])
    for cut in split[1:]:
        factor_of = factor_of * one(*cut)
    return factor_of


def scatter_about(key, dims, deviation, most, pieces=(), kind=jnp.bfloat16):
    array = deviation * jax.random.normal(key, dims, jnp.float32)
    if pieces:
        array = array * level_of(key, dims, pieces, -0.22, 0.18)
    return jnp.clip(array, -most, most).astype(kind)


def setup_inputs(seed: int = 0) -> dict:
    key_of = jax.random.split(jax.random.key(seed), 6)
    measured = scatter_about(key_of[0], (ANGLES, N, 2, N), 1.0, 6.0, ((0, 8), (1, 64)))
    slices = scatter_about(key_of[1], (2, N, 2, N), 0.7, 5.0, ((1, 64), (3, 8)))
    kernel_taps = scatter_about(key_of[2], (2, TAPS), ((2.0 * TAPS) ** -0.5), 1.25)
    angle_freq = jnp.clip(jax.random.uniform(key_of[3], (ANGLES_ALL, 2), jnp.float32, -40.0, 40.0), -40.0, 40.0)
    chosen = set_ends(jax.random.randint(key_of[4], (ANGLES,), 0, ANGLES_ALL), jax.random.fold_in(key_of[4], 1), 0, ANGLES_ALL - 1).astype(jnp.int32)
    return {"measured": measured, "slices": slices, "kernel_taps": kernel_taps, "angle_freq": angle_freq, "chosen": chosen}


def toeplitz(row_taps, out_width):
    tap_count = row_taps.shape[0]
    window = out_width + tap_count - 1
    padded = jnp.concatenate([row_taps, jnp.zeros((out_width,), row_taps.dtype)])
    tiled = jnp.tile(padded, out_width)[: out_width * window]
    return tiled.reshape(out_width, window).T


def kernel_pair(kernel_taps, out_width):
    return jnp.concatenate([toeplitz(kernel_taps[0], out_width), toeplitz(kernel_taps[1], out_width)], axis=1)


def adjoint_taps(kernel_taps):
    return jnp.stack([kernel_taps[0][::-1], -kernel_taps[1][::-1]])


def correlate_columns(field, kernel):
    window, doubled = kernel.shape
    tile_len = doubled // 2
    half_taps = (window - tile_len) // 2
    leading, comps, length = field.shape
    blocks = length // tile_len
    padded = jnp.pad(field, ((0, 0), (0, 0), (half_taps, tile_len - half_taps)))
    main_part = padded[:, :, :length].reshape(leading, comps, blocks, tile_len)
    tail_part = padded[:, :, tile_len:tile_len + length].reshape(leading, comps, blocks, tile_len)[..., : 2 * half_taps]
    windows = jnp.concatenate([main_part, tail_part], axis=3)
    product = jnp.einsum("rpnw,wk->rpnk", windows.astype(jnp.float32), kernel.astype(jnp.float32))
    real_part = product[:, 0, :, :tile_len] - product[:, 1, :, tile_len:]
    imag_part = product[:, 0, :, tile_len:] + product[:, 1, :, :tile_len]
    return jnp.stack([real_part, imag_part], axis=1).reshape(leading, comps, length).astype(jnp.bfloat16)


def correlate_rows(field, kernel):
    window, doubled = kernel.shape
    tile_len = doubled // 2
    half_taps = (window - tile_len) // 2
    leading, comps, length = field.shape
    blocks = leading // tile_len
    padded = jnp.pad(field, ((half_taps, tile_len - half_taps), (0, 0), (0, 0)))
    main_part = padded[:leading].reshape(blocks, tile_len, comps, length)
    tail_part = padded[tile_len:tile_len + leading].reshape(blocks, tile_len, comps, length)[:, : 2 * half_taps]
    windows = jnp.concatenate([main_part, tail_part], axis=1)
    product = jnp.einsum("nwpc,wk->nkpc", windows.astype(jnp.float32), kernel.astype(jnp.float32))
    real_part = product[:, :tile_len, 0] - product[:, tile_len:, 1]
    imag_part = product[:, tile_len:, 0] + product[:, :tile_len, 1]
    return jnp.stack([real_part, imag_part], axis=2).reshape(leading, comps, length).astype(jnp.bfloat16)


def complex_times(left, right):
    left = left.astype(jnp.float32)
    right = right.astype(jnp.float32)
    real_part = left[:, 0] * right[:, 0] - left[:, 1] * right[:, 1]
    imag_part = left[:, 0] * right[:, 1] + left[:, 1] * right[:, 0]
    return jnp.stack([real_part, imag_part], axis=1)


def conjugate_times(left, right):
    left = left.astype(jnp.float32)
    right = right.astype(jnp.float32)
    real_part = left[:, 0] * right[:, 0] + left[:, 1] * right[:, 1]
    imag_part = left[:, 0] * right[:, 1] - left[:, 1] * right[:, 0]
    return jnp.stack([real_part, imag_part], axis=1)


def incident(freq, row_pos, col_pos, length):
    scale = 2.0 * math.pi / length
    phase = scale * (freq[0] * row_pos[:, None] + freq[1] * col_pos[None, :])
    return jnp.stack([jnp.cos(phase), jnp.sin(phase)], axis=1)


def reference(measured, slices, kernel_taps, angle_freq, chosen):
    forward_kernel = kernel_pair(kernel_taps, 128)
    adjoint_kernel = kernel_pair(adjoint_taps(kernel_taps), 128)
    positions = jnp.arange(N).astype(jnp.float32)
    grad_near = jnp.zeros((N, 2, N), jnp.float32)
    grad_far = jnp.zeros((N, 2, N), jnp.float32)
    for member in range(ANGLES):
        freq = angle_freq[chosen[member]]
        entering = incident(freq, positions, positions, N)
        entry0 = complex_times(slices[0], entering).astype(jnp.bfloat16)
        inner = correlate_rows(correlate_columns(entry0, forward_kernel), forward_kernel)
        entry1 = complex_times(slices[1], inner).astype(jnp.bfloat16)
        exit_field = correlate_rows(correlate_columns(entry1, forward_kernel), forward_kernel)
        residue = (exit_field.astype(jnp.float32) - measured[member].astype(jnp.float32)).astype(jnp.bfloat16)
        back_far = correlate_columns(correlate_rows(residue, adjoint_kernel), adjoint_kernel)
        grad_far = grad_far + conjugate_times(inner, back_far)
        carried = conjugate_times(slices[1], back_far).astype(jnp.bfloat16)
        back_near = correlate_columns(correlate_rows(carried, adjoint_kernel), adjoint_kernel)
        grad_near = grad_near + conjugate_times(entering, back_near)
    return grad_near, grad_far
```

```python
import functools
import math

import jax
import jax.numpy as jnp
from jax import lax
from jax.experimental import pallas as pl
from jax.experimental.pallas import tpu as pltpu
from jax.sharding import PartitionSpec as P

MESH = pl.DeviceIdType.MESH
F32 = jnp.float32
BF16 = jnp.bfloat16
ROWS = 32
LANES = 128
UNITS = 9
REACH = 32
TAPS = 65


def build_taps(taps_ref, line, wf, wa, rf, ra):
    line[...] = jnp.zeros_like(line)
    line[0:2, 0:TAPS] = taps_ref[...].astype(F32)
    gr = line[0:1, :]
    gi = line[1:2, :]

    def column(vec, j):
        wide = jnp.broadcast_to(vec, (LANES, 4 * LANES))
        shift = (LANES * (j - 1) - REACH) % (4 * LANES)
        return pltpu.roll(wide, shift, 1, stride=1, stride_axis=0)[:, :LANES]

    for j in range(3):
        re = column(gr, j)
        im = column(gi, j)
        wa[j, 0:LANES, 0:LANES] = re.astype(BF16)
        wa[j, 0:LANES, LANES:] = (-im).astype(BF16)
        wa[j, LANES:, 0:LANES] = im.astype(BF16)
        wa[j, LANES:, LANES:] = re.astype(BF16)
        ret = re.T
        imt = im.T
        wf[2 - j, 0:LANES, 0:LANES] = ret.astype(BF16)
        wf[2 - j, 0:LANES, LANES:] = imt.astype(BF16)
        wf[2 - j, LANES:, 0:LANES] = (-imt).astype(BF16)
        wf[2 - j, LANES:, LANES:] = ret.astype(BF16)

    def row(vec, sign):
        narrow = vec[:, :LANES]
        ahead = pltpu.roll(jnp.broadcast_to(narrow, (ROWS, LANES)), 0, 1, stride=1, stride_axis=0)
        back = pltpu.roll(
            jnp.broadcast_to(narrow, (LANES, LANES)), LANES - 2 * REACH, 1, stride=1, stride_axis=0
        )
        return ahead, sign * back.T[0:ROWS, :]

    fr, br = row(gr, 1.0)
    fi, bi = row(gi, -1.0)
    rf[0:ROWS, :] = fr.astype(BF16)
    rf[ROWS:, :] = fi.astype(BF16)
    ra[0:ROWS, :] = br.astype(BF16)
    ra[ROWS:, :] = bi.astype(BF16)


def row_correlate(taps, window):
    both = jnp.dot(taps[:, 0 : 3 * ROWS], window, preferred_element_type=F32)
    re = both[:ROWS, :LANES] - both[ROWS:, LANES:]
    im = both[:ROWS, LANES:] + both[ROWS:, :LANES]
    return re, im


def times(ar, ai, br, bi):
    return ar * br - ai * bi, ar * bi + ai * br


def conj_times(ar, ai, br, bi):
    return ar * br + ai * bi, ar * bi - ai * br


def join(re, im):
    return jnp.concatenate([re, im], axis=-1)


def parts(value):
    value = value.astype(F32)
    return value[..., :LANES], value[..., LANES:]


def kernel(
    rows_n,
    length,
    chosen_ref,
    table_ref,
    taps_ref,
    near_ref,
    far_ref,
    meas_ref,
    out_near,
    out_far,
    near,
    far,
    other,
    freq,
    other_freq,
    line,
    wf,
    wa,
    rf,
    ra,
    inc,
    inner,
    field,
    halo,
    sum_near,
    sum_far,
    pack_near,
    pack_far,
    got_near,
    got_far,
    slab_send,
    slab_recv,
    edge_send,
    edge_recv,
    pair_send,
    pair_recv,
    halo_send,
    halo_recv,
    grad_send,
    grad_recv,
):
    r = lax.axis_index("rows")
    a = lax.axis_index("ang")
    zh = a // 4
    x = lax.rem(a, 4)
    has_up = r > 0
    has_dn = r < rows_n - 1
    up = lax.rem(r + rows_n - 1, rows_n)
    dn = lax.rem(r + 1, rows_n)
    pair = lax.rem(a + 4, 8)
    mine = zh + 2 * x

    barrier = pltpu.get_barrier_semaphore()
    for k in range(1, 8):
        pl.semaphore_signal(barrier, inc=1, device_id=(r, lax.rem(a + k, 8)), device_id_type=MESH)

    @pl.when(has_up)
    def _():
        pl.semaphore_signal(barrier, inc=1, device_id=(up, a), device_id_type=MESH)

    @pl.when(has_dn)
    def _():
        pl.semaphore_signal(barrier, inc=1, device_id=(dn, a), device_id_type=MESH)

    build_taps(taps_ref, line, wf, wa, rf, ra)
    fy = table_ref[chosen_ref[0], 0]
    fx = table_ref[chosen_ref[0], 1]
    row_id = lax.broadcasted_iota(jnp.int32, (8, LANES), 0)
    freq[...] = jnp.where(row_id < 4, jnp.full((8, LANES), fy, F32), jnp.full((8, LANES), fx, F32))

    base = 7 * zh

    def waves(t, ref):
        vy = ref[0:1, :]
        vx = ref[4:5, :]
        pos_r = (r * ROWS + lax.broadcasted_iota(jnp.int32, (ROWS, LANES), 0)).astype(F32)
        pos_c = (
            (base + lax.broadcasted_iota(jnp.int32, (16, LANES), 0)) * LANES
            + lax.broadcasted_iota(jnp.int32, (16, LANES), 1)
        ).astype(F32)
        turn_r = (vy * pos_r) * (1.0 / length)
        turn_c = (vx * pos_c) * (1.0 / length)
        ang_r = (2.0 * math.pi) * (turn_r - jnp.floor(turn_r + 0.5))
        ang_c = (2.0 * math.pi) * (turn_c - jnp.floor(turn_c + 0.5))
        cr, sr = jnp.cos(ang_r), jnp.sin(ang_r)
        cc, sc = jnp.cos(ang_c), jnp.sin(ang_c)
        for u in range(UNITS):
            re, im = times(cr, sr, cc[u : u + 1, :], sc[u : u + 1, :])
            inc[t, u, :, 0:LANES] = re
            inc[t, u, :, LANES:] = im

    waves(0, freq)
    for t in range(2):
        field[t, 0] = jnp.zeros((ROWS, 2 * LANES), BF16)
        field[t, UNITS + 1] = jnp.zeros((ROWS, 2 * LANES), BF16)

    @pl.when(jnp.logical_not(has_up))
    def _():
        halo[:, :, :, 0:ROWS, :] = jnp.zeros((4, 2, UNITS, ROWS, 2 * LANES), BF16)

    @pl.when(jnp.logical_not(has_dn))
    def _():
        halo[:, :, :, 2 * ROWS :, :] = jnp.zeros((4, 2, UNITS, ROWS, 2 * LANES), BF16)

    near[pl.ds(mine, 2)] = near_ref[...]
    far[pl.ds(mine, 2)] = far_ref[...]

    pl.semaphore_wait(barrier, 7 + has_up.astype(jnp.int32) + has_dn.astype(jnp.int32))

    slabs = ((near_ref, near), (far_ref, far))

    def slab_copy(i, k):
        src, dst = slabs[i]
        return pltpu.make_async_remote_copy(
            src_ref=src,
            dst_ref=dst.at[pl.ds(mine, 2)],
            send_sem=slab_send.at[i, k - 1],
            recv_sem=slab_recv.at[i, k - 1],
            device_id=(r, 4 * zh + lax.rem(x + k, 4)),
            device_id_type=MESH,
        )

    def edge_copy(i, k):
        src, dst = slabs[i]
        return pltpu.make_async_remote_copy(
            src_ref=src.at[pl.ds(1 - zh, 1)],
            dst_ref=dst.at[pl.ds(8 * zh, 1)],
            send_sem=edge_send.at[i, k],
            recv_sem=edge_recv.at[i],
            device_id=(r, 4 * (1 - zh) + k),
            device_id_type=MESH,
        )

    def edge_wait(i):
        src, dst = slabs[i]
        pltpu.make_async_remote_copy(
            src_ref=src.at[pl.ds(0, 1)],
            dst_ref=dst.at[pl.ds(8 * (1 - zh), 1)],
            send_sem=edge_send.at[i, 0],
            recv_sem=edge_recv.at[i],
            device_id=(r, pair),
            device_id_type=MESH,
        ).wait_recv()

    def slab_wait(i):
        for k in range(1, 4):
            slab_copy(i, k).wait_recv()

    freq_copy = pltpu.make_async_remote_copy(
        src_ref=freq,
        dst_ref=other_freq,
        send_sem=pair_send.at[0],
        recv_sem=pair_recv.at[0],
        device_id=(r, pair),
        device_id_type=MESH,
    )
    meas_copy = pltpu.make_async_remote_copy(
        src_ref=meas_ref.at[pl.ds(7 * (1 - zh), UNITS)],
        dst_ref=other,
        send_sem=pair_send.at[1],
        recv_sem=pair_recv.at[1],
        device_id=(r, pair),
        device_id_type=MESH,
    )
    owner = x == 3 * (1 - zh)

    @pl.when(owner)
    def _():
        for k in range(4):
            edge_copy(0, k).start()

    freq_copy.start()
    for k in range(1, 4):
        slab_copy(0, k).start()

    @pl.when(owner)
    def _():
        for k in range(4):
            edge_copy(1, k).start()

    for k in range(1, 4):
        slab_copy(1, k).start()
    meas_copy.start()

    def halo_copy(s, t, down):
        lo = 0 if down else 2 * ROWS
        i = 0 if down else 1
        return pltpu.make_async_remote_copy(
            src_ref=halo.at[s, t, :, ROWS : 2 * ROWS, :],
            dst_ref=halo.at[s, t, :, lo : lo + ROWS, :],
            send_sem=halo_send.at[s, t, i],
            recv_sem=halo_recv.at[s, t, i],
            device_id=(dn if down else up, a),
            device_id_type=MESH,
        )

    def halo_start(s, t):
        @pl.when(has_dn)
        def _():
            halo_copy(s, t, True).start()

        @pl.when(has_up)
        def _():
            halo_copy(s, t, False).start()

    def halo_wait(s, t):
        @pl.when(has_up)
        def _():
            halo_copy(s, t, True).wait_recv()

        @pl.when(has_dn)
        def _():
            halo_copy(s, t, False).wait_recv()

    def halo_done(s, t):
        @pl.when(has_dn)
        def _():
            halo_copy(s, t, True).wait_send()

        @pl.when(has_up)
        def _():
            halo_copy(s, t, False).wait_send()

    def each_unit(body):
        def step(u, carry):
            body(u)
            return carry

        lax.fori_loop(0, UNITS, step, 0, unroll=3)

    def columns(t, w, body):
        def step(c, carry):
            acc = None
            for j in range(3):
                lhs = field[t, pl.ds(3 * c + j, 3)].reshape(3 * ROWS, 2 * LANES)
                term = jnp.dot(lhs, w[j], preferred_element_type=F32)
                acc = term if acc is None else acc + term
            body(3 * c, acc.astype(BF16).reshape(3, ROWS, 2 * LANES))
            return carry

        lax.fori_loop(0, 3, step, 0)

    def own(s, t, u, value):
        halo[s, t, pl.ds(u, 3), ROWS : 2 * ROWS, :] = value

    def enter(t):
        def body(u):
            re, im = times(*parts(near[u]), *parts(inc[t, u]))
            field[t, u + 1] = join(re, im).astype(BF16)

        each_unit(body)
        columns(t, wf, lambda u, value: own(0, t, u, value))
        halo_start(0, t)

    def second(t):
        halo_wait(0, t)

        def body(u):
            re, im = row_correlate(rf, halo[0, t, u])
            value = join(re, im).astype(BF16)
            inner[t, u] = value
            re, im = times(*parts(far[u]), *parts(value))
            field[t, u + 1] = join(re, im).astype(BF16)

        each_unit(body)
        columns(t, wf, lambda u, value: own(1, t, u, value))
        halo_start(1, t)

    def compare(t, target):
        halo_wait(1, t)

        def body(u):
            re, im = row_correlate(rf, halo[1, t, u])
            value = join(re, im).astype(BF16)
            diff = value.astype(F32) - target(u).astype(F32)
            halo[2, t, u, ROWS : 2 * ROWS, :] = diff.astype(BF16)

        each_unit(body)
        halo_start(2, t)

    def back(s, t):
        halo_wait(s, t)

        def body(u):
            re, im = row_correlate(ra, halo[s, t, u])
            field[t, u + 1] = join(re, im).astype(BF16)

        each_unit(body)

    def back_far(t):
        back(2, t)

        def body(u, value):
            br, bi = parts(value)
            gr, gi = conj_times(*parts(inner[t, pl.ds(u, 3)]), br, bi)
            grad = join(gr, gi)
            if t == 0:
                sum_far[pl.ds(u, 3)] = grad
            else:
                grad = grad + sum_far[pl.ds(u, 3)]
                sum_far[pl.ds(u, 3)] = grad
                pack_far[pl.ds(u, 3)] = grad.astype(BF16)
            re, im = conj_times(*parts(far[pl.ds(u, 3)]), br, bi)
            own(3, t, u, join(re, im).astype(BF16))

        columns(t, wa, body)
        halo_start(3, t)

    def back_near(t):
        back(3, t)

        def body(u, value):
            gr, gi = conj_times(*parts(inc[t, pl.ds(u, 3)]), *parts(value))
            grad = join(gr, gi)
            if t == 0:
                sum_near[pl.ds(u, 3)] = grad
            else:
                grad = grad + sum_near[pl.ds(u, 3)]
                sum_near[pl.ds(u, 3)] = grad
                pack_near[pl.ds(u, 3)] = grad.astype(BF16)

        columns(t, wa, body)

    grads = ((pack_near, got_near), (pack_far, got_far))

    def grad_copy(i, k):
        src, dst = grads[i]
        to = lax.rem(x + k, 4)
        return pltpu.make_async_remote_copy(
            src_ref=src.at[pl.ds(zh + 2 * to, 2)],
            dst_ref=dst.at[k - 1],
            send_sem=grad_send.at[i, k - 1],
            recv_sem=grad_recv.at[i, k - 1],
            device_id=(r, 4 * zh + to),
            device_id_type=MESH,
        )

    slab_wait(0)
    edge_wait(0)
    enter(0)
    freq_copy.wait_recv()
    waves(1, other_freq)
    enter(1)
    slab_wait(1)
    edge_wait(1)
    second(0)
    second(1)
    compare(0, lambda u: meas_ref[7 * zh + u])
    meas_copy.wait_recv()
    compare(1, lambda u: other[u])
    back_far(0)
    back_far(1)
    for k in range(1, 4):
        grad_copy(1, k).start()
    back_near(0)
    back_near(1)
    for k in range(1, 4):
        grad_copy(0, k).start()

    def finish(i, total, got, out):
        for k in range(1, 4):
            grad_copy(i, k).wait_recv()
        value = total[pl.ds(mine, 2)]
        for k in range(3):
            value = value + got[k].astype(F32)
        out[...] = value

    finish(1, sum_far, got_far, out_far)
    finish(0, sum_near, got_near, out_near)

    for i in range(2):
        for k in range(1, 4):
            slab_copy(i, k).wait_send()
            grad_copy(i, k).wait_send()

        @pl.when(owner)
        def _():
            for k in range(4):
                edge_copy(i, k).wait_send()

    freq_copy.wait_send()
    meas_copy.wait_send()
    for s in range(4):
        for t in range(2):
            halo_done(s, t)


def local(rows_n, measured, slices, kernel_taps, angle_freq, chosen):
    length = measured.shape[3]
    blocks = length // LANES
    meas = measured[0].reshape(ROWS, 2, blocks, LANES).transpose(2, 0, 1, 3)
    meas = meas.reshape(blocks, ROWS, 2 * LANES)
    slabs = slices.reshape(2, ROWS, 2, 2, LANES).transpose(0, 3, 1, 2, 4)
    slabs = slabs.reshape(2, 2, ROWS, 2 * LANES)
    unit = (ROWS, 2 * LANES)
    vmem = pl.BlockSpec(memory_space=pltpu.VMEM)
    smem = pl.BlockSpec(memory_space=pltpu.SMEM)
    dma = pltpu.SemaphoreType.DMA
    out = jax.ShapeDtypeStruct((2,) + unit, F32)
    grad_near, grad_far = pl.pallas_call(
        functools.partial(kernel, rows_n, length),
        out_shape=(out, out),
        in_specs=[smem, smem, vmem, vmem, vmem, vmem],
        out_specs=(vmem, vmem),
        scratch_shapes=[
            pltpu.VMEM((UNITS,) + unit, BF16),
            pltpu.VMEM((UNITS,) + unit, BF16),
            pltpu.VMEM((UNITS,) + unit, BF16),
            pltpu.VMEM((8, LANES), F32),
            pltpu.VMEM((8, LANES), F32),
            pltpu.VMEM((8, 4 * LANES), F32),
            pltpu.VMEM((3, 2 * LANES, 2 * LANES), BF16),
            pltpu.VMEM((3, 2 * LANES, 2 * LANES), BF16),
            pltpu.VMEM((2 * ROWS, LANES), BF16),
            pltpu.VMEM((2 * ROWS, LANES), BF16),
            pltpu.VMEM((2, UNITS) + unit, F32),
            pltpu.VMEM((2, UNITS) + unit, BF16),
            pltpu.VMEM((2, UNITS + 2) + unit, BF16),
            pltpu.VMEM((4, 2, UNITS, 3 * ROWS, 2 * LANES), BF16),
            pltpu.VMEM((UNITS,) + unit, F32),
            pltpu.VMEM((UNITS,) + unit, F32),
            pltpu.VMEM((UNITS,) + unit, BF16),
            pltpu.VMEM((UNITS,) + unit, BF16),
            pltpu.VMEM((3, 2) + unit, BF16),
            pltpu.VMEM((3, 2) + unit, BF16),
            dma((2, 3)),
            dma((2, 3)),
            dma((2, 4)),
            dma((2,)),
            dma((2,)),
            dma((2,)),
            dma((4, 2, 2)),
            dma((4, 2, 2)),
            dma((2, 3)),
            dma((2, 3)),
        ],
        compiler_params=pltpu.CompilerParams(collective_id=0, has_side_effects=True),
    )(chosen, angle_freq, kernel_taps, slabs[0], slabs[1], meas)

    def place(grad):
        return grad.reshape(2, ROWS, 2, LANES).transpose(1, 2, 0, 3).reshape(ROWS, 2, 2 * LANES)

    return place(grad_near), place(grad_far)


def solution(mesh):
    return jax.shard_map(
        functools.partial(local, mesh.shape["rows"]),
        mesh=mesh,
        in_specs=(P("ang", "rows", None, None), P(None, "rows", None, "ang"), P(), P(), P("ang")),
        out_specs=(P("rows", None, "ang"), P("rows", None, "ang")),
        check_vma=False,
    )
```

```python
import functools
import math

import jax
import jax.numpy as jnp
from jax import lax
from jax.experimental import pallas as pl
from jax.experimental.pallas import tpu as pltpu
from jax.sharding import PartitionSpec as P

MESH = pl.DeviceIdType.MESH
F32 = jnp.float32
BF16 = jnp.bfloat16
ROWS = 32
LANES = 128
UNITS = 9
REACH = 32
TAPS = 65


def build_taps(zh, taps_ref, line, wf, wa, rf, ra):
    line[...] = jnp.zeros_like(line)
    line[0:2, 0:TAPS] = taps_ref[...].astype(F32)
    gr = line[0:1, :]
    gi = line[1:2, :]

    def column(vec, j):
        wide = jnp.broadcast_to(vec, (LANES, 4 * LANES))
        shift = (LANES * (j - 1) - REACH) % (4 * LANES)
        return pltpu.roll(wide, shift, 1, stride=1, stride_axis=0)[:, :LANES]

    for j in range(3):
        re = column(gr, j)
        im = column(gi, j)
        ja = j + zh * (2 - 2 * j)
        jf = 2 - ja
        wa[ja, 0:LANES, 0:LANES] = re.astype(BF16)
        wa[ja, 0:LANES, LANES:] = (-im).astype(BF16)
        wa[ja, LANES:, 0:LANES] = im.astype(BF16)
        wa[ja, LANES:, LANES:] = re.astype(BF16)
        ret = re.T
        imt = im.T
        wf[jf, 0:LANES, 0:LANES] = ret.astype(BF16)
        wf[jf, 0:LANES, LANES:] = imt.astype(BF16)
        wf[jf, LANES:, 0:LANES] = (-imt).astype(BF16)
        wf[jf, LANES:, LANES:] = ret.astype(BF16)

    def row(vec, sign):
        narrow = vec[:, :LANES]
        ahead = pltpu.roll(jnp.broadcast_to(narrow, (ROWS, LANES)), 0, 1, stride=1, stride_axis=0)
        back = pltpu.roll(
            jnp.broadcast_to(narrow, (LANES, LANES)), LANES - 2 * REACH, 1, stride=1, stride_axis=0
        )
        return ahead, sign * back.T[0:ROWS, :]

    fr, br = row(gr, 1.0)
    fi, bi = row(gi, -1.0)
    rf[0:ROWS, :] = fr.astype(BF16)
    rf[ROWS:, :] = fi.astype(BF16)
    ra[0:ROWS, :] = br.astype(BF16)
    ra[ROWS:, :] = bi.astype(BF16)


def row_correlate(taps, window):
    both = jnp.dot(taps[:, 0 : 3 * ROWS], window, preferred_element_type=F32)
    re = both[:ROWS, :LANES] - both[ROWS:, LANES:]
    im = both[:ROWS, LANES:] + both[ROWS:, :LANES]
    return re, im


def times(ar, ai, br, bi):
    return ar * br - ai * bi, ar * bi + ai * br


def conj_times(ar, ai, br, bi):
    return ar * br + ai * bi, ar * bi - ai * br


def join(re, im):
    return jnp.concatenate([re, im], axis=-1)


def parts(value):
    value = value.astype(F32)
    return value[..., :LANES], value[..., LANES:]


PARTS = (((0, 7), (7, 9)), ((0, 6), (6, 9)), ((0, 3), (3, 6), (6, 9)), ((0, 3), (3, 6), (6, 9)))
PIECE = 3 * LANES


def kernel(
    rows_n,
    length,
    chosen_ref,
    table_ref,
    taps_ref,
    slices_ref,
    meas_ref,
    out_near,
    out_far,
    slab_raw,
    slab_wide,
    meas_raw,
    meas_wide,
    near,
    far,
    freq,
    other_freq,
    line,
    wf,
    wa,
    rf,
    ra,
    inc,
    inner,
    field,
    halo,
    sum_near,
    sum_far,
    pack_near,
    pack_far,
    got_near,
    got_far,
    load_sem,
    slab_send,
    slab_recv,
    edge_send,
    edge_recv,
    relay_send,
    relay_recv,
    freq_send,
    freq_recv,
    meas_send,
    meas_recv,
    halo_send,
    halo_recv,
    grad_send,
    grad_recv,
):
    r = lax.axis_index("rows")
    a = lax.axis_index("ang")
    zh = a // 4
    x = lax.rem(a, 4)
    has_up = r > 0
    has_dn = r < rows_n - 1
    up = lax.rem(r + rows_n - 1, rows_n)
    dn = lax.rem(r + 1, rows_n)
    pair = lax.rem(a + 4, 8)

    def first_of(other_x):
        return 2 * other_x + zh * (6 - 4 * other_x)

    mine = first_of(x)

    def flip(i, n):
        return i + zh * (n - 1 - 2 * i)

    barrier = pltpu.get_barrier_semaphore()
    pl.semaphore_signal(barrier, inc=1, device_id=(r, pair), device_id_type=MESH)
    for k in range(1, 4):
        to = (r, 4 * zh + lax.rem(x + k, 4))
        pl.semaphore_signal(barrier, inc=1, device_id=to, device_id_type=MESH)

    @pl.when(has_up)
    def _():
        pl.semaphore_signal(barrier, inc=1, device_id=(up, a), device_id_type=MESH)

    @pl.when(has_dn)
    def _():
        pl.semaphore_signal(barrier, inc=1, device_id=(dn, a), device_id_type=MESH)

    def piece_of(half, c):
        first = 7 * half + 3 * c + half * (6 - 6 * c)
        return meas_ref.at[0, :, :, pl.ds(pl.multiple_of(first * LANES, LANES), PIECE)]

    slab_load = pltpu.make_async_copy(slices_ref, slab_raw, load_sem.at[0])
    slab_load.start()
    meas_loads = [
        pltpu.make_async_copy(piece_of(zh, c), meas_raw.at[0, c], load_sem.at[1 + c])
        for c in range(3)
    ]
    for load in meas_loads:
        load.start()

    fy = table_ref[0, chosen_ref[0]]
    fx = table_ref[1, chosen_ref[0]]
    freq[0:1, :] = jnp.full((1, LANES), fy, F32)
    freq[1:2, :] = jnp.full((1, LANES), fx, F32)

    slab_load.wait()
    slabs = (near, far)
    for i in range(2):
        slab_wide[...] = slab_raw[i].astype(F32)
        for k in range(2):
            lanes = slice(k * LANES, (k + 1) * LANES)
            unit = join(slab_wide[:, 0, lanes], slab_wide[:, 1, lanes])
            slabs[i][mine + flip(k, 2)] = unit.astype(BF16)

    build_taps(zh, taps_ref, line, wf, wa, rf, ra)

    def waves(t, ref):
        vy = ref[0:1, :]
        vx = ref[1:2, :]
        unit = lax.broadcasted_iota(jnp.int32, (16, LANES), 0)
        pos_r = (r * ROWS + lax.broadcasted_iota(jnp.int32, (ROWS, LANES), 0)).astype(F32)
        pos_c = (flip(unit, 16) * LANES + lax.broadcasted_iota(jnp.int32, (16, LANES), 1)).astype(F32)
        turn_r = (vy * pos_r) * (1.0 / length)
        turn_c = (vx * pos_c) * (1.0 / length)
        ang_r = (2.0 * math.pi) * (turn_r - jnp.floor(turn_r + 0.5))
        ang_c = (2.0 * math.pi) * (turn_c - jnp.floor(turn_c + 0.5))
        cr, sr = jnp.cos(ang_r), jnp.sin(ang_r)
        cc, sc = jnp.cos(ang_c), jnp.sin(ang_c)
        for u in range(UNITS):
            re, im = times(cr, sr, cc[u : u + 1, :], sc[u : u + 1, :])
            inc[t, u, :, 0:LANES] = re
            inc[t, u, :, LANES:] = im

    waves(0, freq)
    for t in range(4):
        field[t, 0] = jnp.zeros((ROWS, 2 * LANES), BF16)
        field[t, UNITS + 1] = jnp.zeros((ROWS, 2 * LANES), BF16)

    @pl.when(jnp.logical_not(has_up))
    def _():
        halo[:, :, :, 0:ROWS, :] = jnp.zeros((4, 2, UNITS, ROWS, 2 * LANES), BF16)

    @pl.when(jnp.logical_not(has_dn))
    def _():
        halo[:, :, :, 2 * ROWS :, :] = jnp.zeros((4, 2, UNITS, ROWS, 2 * LANES), BF16)

    for load in meas_loads:
        load.wait()

    pl.semaphore_wait(barrier, 4 + has_up.astype(jnp.int32) + has_dn.astype(jnp.int32))

    def remote(src, dst, send_sem, recv_sem, to):
        return pltpu.make_async_remote_copy(
            src_ref=src,
            dst_ref=dst,
            send_sem=send_sem,
            recv_sem=recv_sem,
            device_id=to,
            device_id_type=MESH,
        )

    def slab_copy(i, k):
        block = slabs[i].at[pl.ds(mine, 2)]
        to = (r, 4 * zh + lax.rem(x + k, 4))
        return remote(block, block, slab_send.at[i, k - 1], slab_recv.at[i, k - 1], to)

    def slab_wait(i, k):
        block = slabs[i].at[pl.ds(first_of(lax.rem(x + 4 - k, 4)), 2)]
        remote(block, block, slab_send.at[i, k - 1], slab_recv.at[i, k - 1], (r, pair)).wait_recv()

    edges = [
        remote(slabs[i].at[7], slabs[i].at[8], edge_send.at[i], edge_recv.at[i], (r, pair))
        for i in range(2)
    ]
    freq_copy = remote(freq, other_freq, freq_send, freq_recv, (r, pair))
    meas_copies = [
        remote(piece_of(1 - zh, c), meas_raw.at[1, c], meas_send.at[c], meas_recv.at[c], (r, pair))
        for c in range(3)
    ]

    owner = mine == 6
    relay = mine == 0

    def relay_copy(i, k):
        to = (r, 4 * zh + lax.rem(x + k, 4))
        margin = slabs[i].at[8]
        return remote(margin, margin, relay_send.at[i, k - 1], relay_recv.at[i], to)

    def margin_wait(i):
        @pl.when(jnp.logical_not(relay))
        def _():
            relay_copy(i, 1).wait_recv()

    def meas_start():
        for copy in meas_copies:
            copy.start()

    freq_copy.start()

    @pl.when(owner)
    def _():
        edges[0].start()
        edges[1].start()

    for k in range(1, 4):
        slab_copy(0, k).start()
    pl.when(jnp.logical_not(owner))(meas_start)
    for k in range(1, 4):
        slab_copy(1, k).start()

    def halo_copy(s, t, c, down):
        lo = 0 if down else 2 * ROWS
        i = 0 if down else 1
        u0, u1 = PARTS[s][c]
        return remote(
            halo.at[s, t, u0:u1, ROWS : 2 * ROWS, :],
            halo.at[s, t, u0:u1, lo : lo + ROWS, :],
            halo_send.at[s, t, c, i],
            halo_recv.at[s, t, c, i],
            (dn if down else up, a),
        )

    def halo_start(s, t, c):
        @pl.when(has_dn)
        def _():
            halo_copy(s, t, c, True).start()

        @pl.when(has_up)
        def _():
            halo_copy(s, t, c, False).start()

    def halo_wait(s, t, c):
        @pl.when(has_up)
        def _():
            halo_copy(s, t, c, True).wait_recv()

        @pl.when(has_dn)
        def _():
            halo_copy(s, t, c, False).wait_recv()

    def halo_done(s, t, c):
        @pl.when(has_dn)
        def _():
            halo_copy(s, t, c, True).wait_send()

        @pl.when(has_up)
        def _():
            halo_copy(s, t, c, False).wait_send()

    def columns(t, w, u0, u1):
        acc = None
        for j in range(3):
            lhs = field[t, u0 + j : u1 + j].reshape((u1 - u0) * ROWS, 2 * LANES)
            term = jnp.dot(lhs, w[j], preferred_element_type=F32)
            acc = term if acc is None else acc + term
        return acc.astype(BF16).reshape(u1 - u0, ROWS, 2 * LANES)

    def own(s, t, u0, u1, value):
        halo[s, t, u0:u1, ROWS : 2 * ROWS, :] = value

    def enter(t, units, groups, c):
        for u in range(*units):
            re, im = times(*parts(near[u]), *parts(inc[t, u]))
            field[2 + t, u + 1] = join(re, im).astype(BF16)
        for u0, u1 in groups:
            own(0, t, u0, u1, columns(2 + t, wf, u0, u1))
        halo_start(0, t, c)

    def second(t, groups, c):
        halo_wait(0, t, c)
        for u in range(*PARTS[0][c]):
            re, im = row_correlate(rf, halo[0, t, u])
            value = join(re, im).astype(BF16)
            inner[t, u] = value
            re, im = times(*parts(far[u]), *parts(value))
            field[t, u + 1] = join(re, im).astype(BF16)
        for u0, u1 in groups:
            own(1, t, u0, u1, columns(t, wf, u0, u1))
        halo_start(1, t, c)

    def compare(t, c):
        meas_wide[...] = meas_raw[t, c].astype(F32)
        for k in range(3):
            u = 3 * c + k
            re, im = row_correlate(rf, halo[1, t, u])
            value = join(re, im).astype(BF16)
            lanes = pl.ds(pl.multiple_of(flip(k, 3) * LANES, LANES), LANES)
            target = join(meas_wide[:, 0, lanes], meas_wide[:, 1, lanes])
            halo[2, t, u, ROWS : 2 * ROWS, :] = (value.astype(F32) - target).astype(BF16)
        halo_start(2, t, c)

    def back(s, t, c):
        halo_wait(s, t, c)
        for u in range(*PARTS[s][c]):
            re, im = row_correlate(ra, halo[s, t, u])
            field[t, u + 1] = join(re, im).astype(BF16)

    def add(t, total, pack, u0, u1, re, im):
        grad = join(re, im)
        if t == 0:
            total[u0:u1] = grad
        else:
            grad = grad + total[u0:u1]
            total[u0:u1] = grad
            pack[u0:u1] = grad.astype(BF16)

    def back_far(t):
        def piece(c):
            u0, u1 = PARTS[3][c]
            br, bi = parts(columns(t, wa, u0, u1))
            re, im = conj_times(*parts(far[u0:u1]), br, bi)
            own(3, t, u0, u1, join(re, im).astype(BF16))
            halo_start(3, t, c)
            re, im = conj_times(*parts(inner[t, u0:u1]), br, bi)
            add(t, sum_far, pack_far, u0, u1, re, im)

        back(2, t, 0)
        back(2, t, 1)
        piece(0)
        back(2, t, 2)
        piece(1)
        piece(2)

    def back_near(t):
        def piece(c):
            u0, u1 = PARTS[3][c]
            br, bi = parts(columns(t, wa, u0, u1))
            re, im = conj_times(*parts(inc[t, u0:u1]), br, bi)
            add(t, sum_near, pack_near, u0, u1, re, im)

        back(3, t, 0)
        back(3, t, 1)
        piece(0)
        back(3, t, 2)
        piece(1)
        piece(2)

    grads = ((pack_near, got_near, sum_near, out_near), (pack_far, got_far, sum_far, out_far))

    def grad_copy(i, k):
        to = lax.rem(x + k, 4)
        src = grads[i][0].at[pl.ds(first_of(to), 2)]
        dst = grads[i][1].at[k - 1]
        return remote(src, dst, grad_send.at[i, k - 1], grad_recv.at[i, k - 1], (r, 4 * zh + to))

    def finish(i):
        _, got, total, out = grads[i]
        for k in range(1, 4):
            grad_copy(i, k).wait_recv()
        for j in range(2):
            at = flip(j, 2)
            value = total[mine + at]
            for k in range(3):
                value = value + got[k, at].astype(F32)
            out[:, 0, j * LANES : (j + 1) * LANES] = value[:, :LANES]
            out[:, 1, j * LANES : (j + 1) * LANES] = value[:, LANES:]

    early = ((0, 4), (4, 7))
    for k in range(1, 4):
        slab_wait(0, k)
    pl.when(owner)(meas_start)
    enter(0, (0, 8), early, 0)
    freq_copy.wait_recv()
    waves(1, other_freq)
    enter(1, (0, 8), early, 0)

    @pl.when(relay)
    def _():
        for i in range(2):
            edges[i].wait_recv()
            for k in range(1, 4):
                relay_copy(i, k).start()

    for k in range(1, 4):
        slab_wait(1, k)
    early = ((0, 3), (3, 6))
    second(0, early, 0)
    margin_wait(0)
    enter(0, (8, 9), ((7, 9),), 1)
    enter(1, (8, 9), ((7, 9),), 1)
    second(1, early, 0)
    margin_wait(1)
    second(0, ((6, 9),), 1)
    second(1, ((6, 9),), 1)
    halo_wait(1, 0, 0)
    compare(0, 0)
    compare(0, 1)
    halo_wait(1, 1, 0)
    for c in range(2):
        meas_copies[c].wait_recv()
        compare(1, c)
    halo_wait(1, 0, 1)
    compare(0, 2)
    halo_wait(1, 1, 1)
    meas_copies[2].wait_recv()
    compare(1, 2)
    back_far(0)
    back_far(1)
    for k in range(1, 4):
        grad_copy(1, k).start()
    back_near(0)
    back_near(1)
    for k in range(1, 4):
        grad_copy(0, k).start()
    finish(1)
    finish(0)

    for i in range(2):
        for k in range(1, 4):
            slab_copy(i, k).wait_send()
            grad_copy(i, k).wait_send()

        @pl.when(owner)
        def _():
            edges[i].wait_send()

        @pl.when(relay)
        def _():
            for k in range(1, 4):
                relay_copy(i, k).wait_send()

    freq_copy.wait_send()
    for copy in meas_copies:
        copy.wait_send()
    for s in range(4):
        for t in range(2):
            for c in range(len(PARTS[s])):
                halo_done(s, t, c)


def local(rows_n, measured, slices, kernel_taps, angle_freq, chosen):
    length = measured.shape[3]
    unit = (ROWS, 2 * LANES)
    vmem = pl.BlockSpec(memory_space=pltpu.VMEM)
    smem = pl.BlockSpec(memory_space=pltpu.SMEM)
    place = pl.BlockSpec(memory_space=pl.ANY)
    dma = pltpu.SemaphoreType.DMA
    out = jax.ShapeDtypeStruct((ROWS, 2, 2 * LANES), F32)
    return pl.pallas_call(
        functools.partial(kernel, rows_n, length),
        out_shape=(out, out),
        in_specs=[smem, smem, vmem, place, place],
        out_specs=(vmem, vmem),
        scratch_shapes=[
            pltpu.VMEM((2, ROWS, 2, 2 * LANES), BF16),
            pltpu.VMEM((ROWS, 2, 2 * LANES), F32),
            pltpu.VMEM((2, 3, ROWS, 2, PIECE), BF16),
            pltpu.VMEM((ROWS, 2, PIECE), F32),
            pltpu.VMEM((UNITS,) + unit, BF16),
            pltpu.VMEM((UNITS,) + unit, BF16),
            pltpu.VMEM((2, LANES), F32),
            pltpu.VMEM((2, LANES), F32),
            pltpu.VMEM((8, 4 * LANES), F32),
            pltpu.VMEM((3, 2 * LANES, 2 * LANES), BF16),
            pltpu.VMEM((3, 2 * LANES, 2 * LANES), BF16),
            pltpu.VMEM((2 * ROWS, LANES), BF16),
            pltpu.VMEM((2 * ROWS, LANES), BF16),
            pltpu.VMEM((2, UNITS) + unit, F32),
            pltpu.VMEM((2, UNITS) + unit, BF16),
            pltpu.VMEM((4, UNITS + 2) + unit, BF16),
            pltpu.VMEM((4, 2, UNITS, 3 * ROWS, 2 * LANES), BF16),
            pltpu.VMEM((UNITS,) + unit, F32),
            pltpu.VMEM((UNITS,) + unit, F32),
            pltpu.VMEM((UNITS,) + unit, BF16),
            pltpu.VMEM((UNITS,) + unit, BF16),
            pltpu.VMEM((3, 2) + unit, BF16),
            pltpu.VMEM((3, 2) + unit, BF16),
            dma((4,)),
            dma((2, 3)),
            dma((2, 3)),
            dma((2,)),
            dma((2,)),
            dma((2, 3)),
            dma((2,)),
            dma,
            dma,
            dma((3,)),
            dma((3,)),
            dma((4, 2, 3, 2)),
            dma((4, 2, 3, 2)),
            dma((2, 3)),
            dma((2, 3)),
        ],
        compiler_params=pltpu.CompilerParams(collective_id=0, has_side_effects=True),
    )(chosen, angle_freq.T, kernel_taps, slices, measured)


def solution(mesh):
    return jax.shard_map(
        functools.partial(local, mesh.shape["rows"]),
        mesh=mesh,
        in_specs=(P("ang", "rows", None, None), P(None, "rows", None, "ang"), P(), P(), P("ang")),
        out_specs=(P("rows", None, "ang"), P("rows", None, "ang")),
        check_vma=False,
    )
```

```python
import functools
import math

import jax
import jax.numpy as jnp
from jax import lax
from jax.experimental import pallas as pl
from jax.experimental.pallas import tpu as pltpu
from jax.sharding import PartitionSpec as P

MESH = pl.DeviceIdType.MESH
F32 = jnp.float32
BF16 = jnp.bfloat16
ROWS = 32
LANES = 128
UNITS = 9
REACH = 32
TAPS = 65


def build_taps(zh, taps_ref, line, wf, wa, rf, ra):
    line[...] = jnp.zeros_like(line)
    line[0:2, 0:TAPS] = taps_ref[...].astype(F32)
    gr = line[0:1, :]
    gi = line[1:2, :]

    def column(vec, j):
        wide = jnp.broadcast_to(vec, (LANES, 4 * LANES))
        shift = (LANES * (j - 1) - REACH) % (4 * LANES)
        return pltpu.roll(wide, shift, 1, stride=1, stride_axis=0)[:, :LANES]

    for j in range(3):
        re = column(gr, j)
        im = column(gi, j)
        ja = j + zh * (2 - 2 * j)
        jf = 2 - ja
        wa[ja, 0:LANES, 0:LANES] = re.astype(BF16)
        wa[ja, 0:LANES, LANES:] = (-im).astype(BF16)
        wa[ja, LANES:, 0:LANES] = im.astype(BF16)
        wa[ja, LANES:, LANES:] = re.astype(BF16)
        ret = re.T
        imt = im.T
        wf[jf, 0:LANES, 0:LANES] = ret.astype(BF16)
        wf[jf, 0:LANES, LANES:] = imt.astype(BF16)
        wf[jf, LANES:, 0:LANES] = (-imt).astype(BF16)
        wf[jf, LANES:, LANES:] = ret.astype(BF16)

    def row(vec, sign):
        narrow = vec[:, :LANES]
        ahead = pltpu.roll(jnp.broadcast_to(narrow, (ROWS, LANES)), 0, 1, stride=1, stride_axis=0)
        back = pltpu.roll(
            jnp.broadcast_to(narrow, (LANES, LANES)), LANES - 2 * REACH, 1, stride=1, stride_axis=0
        )
        return ahead, sign * back.T[0:ROWS, :]

    fr, br = row(gr, 1.0)
    fi, bi = row(gi, -1.0)
    rf[0:ROWS, :] = fr.astype(BF16)
    rf[ROWS:, :] = fi.astype(BF16)
    ra[0:ROWS, :] = br.astype(BF16)
    ra[ROWS:, :] = bi.astype(BF16)


def row_correlate(taps, window):
    both = jnp.dot(taps[:, 0 : 3 * ROWS], window, preferred_element_type=F32)
    re = both[:ROWS, :LANES] - both[ROWS:, LANES:]
    im = both[:ROWS, LANES:] + both[ROWS:, :LANES]
    return re, im


def times(ar, ai, br, bi):
    return ar * br - ai * bi, ar * bi + ai * br


def conj_times(ar, ai, br, bi):
    return ar * br + ai * bi, ar * bi - ai * br


def join(re, im):
    return jnp.concatenate([re, im], axis=-1)


def parts(value):
    value = value.astype(F32)
    return value[..., :LANES], value[..., LANES:]


SLAB_PARTS = ((0, 8),)
PARTS = ((0, 3), (3, 6), (6, 9))
PIECE = 3 * LANES


def kernel(
    rows_n,
    length,
    chosen_ref,
    table_ref,
    taps_ref,
    slices_ref,
    meas_ref,
    out,
    slab_raw,
    slab_wide,
    meas_raw,
    meas_wide,
    near,
    far,
    freq,
    other_freq,
    line,
    wf,
    wa,
    rf,
    ra,
    inc,
    inner,
    entry,
    first,
    field,
    halo,
    sum_near,
    sum_far,
    pack_near,
    pack_far,
    got_near,
    got_far,
    load_sem,
    slab_send,
    slab_recv,
    edge_send,
    edge_recv,
    relay_send,
    relay_recv,
    freq_send,
    freq_recv,
    meas_send,
    meas_recv,
    halo_send,
    halo_recv,
    grad_send,
    grad_recv,
):
    r = lax.axis_index("rows")
    a = lax.axis_index("ang")
    zh = a // 4
    x = lax.rem(a, 4)
    has_up = r > 0
    has_dn = r < rows_n - 1
    up = lax.rem(r + rows_n - 1, rows_n)
    dn = lax.rem(r + 1, rows_n)
    pair = lax.rem(a + 4, 8)

    def first_of(other_x):
        return 2 * other_x + zh * (6 - 4 * other_x)

    mine = first_of(x)

    def flip(i, n):
        return i + zh * (n - 1 - 2 * i)

    barrier = pltpu.get_barrier_semaphore()
    pl.semaphore_signal(barrier, inc=1, device_id=(r, pair), device_id_type=MESH)
    for k in range(1, 4):
        to = (r, 4 * zh + lax.rem(x + k, 4))
        pl.semaphore_signal(barrier, inc=1, device_id=to, device_id_type=MESH)

    owner = mine == 6
    relay = mine == 0
    end = jnp.logical_or(owner, relay)
    for has, row in ((has_up, up), (has_dn, dn)):

        @pl.when(has)
        def _():
            pl.semaphore_signal(barrier, inc=1, device_id=(row, a), device_id_type=MESH)

        @pl.when(jnp.logical_and(has, end))
        def _():
            pl.semaphore_signal(barrier, inc=1, device_id=(row, pair), device_id_type=MESH)

    def meas_from(half, u):
        block = u + half * (15 - 2 * u)
        return meas_ref.at[0, :, :, pl.ds(pl.multiple_of(block * LANES, LANES), LANES)]

    def meas_to(t, u):
        return meas_raw.at[t, u // 3, :, :, u % 3 * LANES : (u % 3 + 1) * LANES]

    slab_load = pltpu.make_async_copy(slices_ref, slab_raw, load_sem.at[0])
    slab_load.start()
    meas_loads = [
        pltpu.make_async_copy(meas_from(zh, u), meas_to(0, u), load_sem.at[1 + u])
        for u in range(UNITS)
    ]
    for load in meas_loads:
        load.start()

    fy = table_ref[0, chosen_ref[0]]
    fx = table_ref[1, chosen_ref[0]]
    freq[0:1, :] = jnp.full((1, LANES), fy, F32)
    freq[1:2, :] = jnp.full((1, LANES), fx, F32)

    slab_load.wait()

    def slab(i, unit, n):
        if i == 0:
            return near.at[pl.ds(unit, n), ROWS : 2 * ROWS, :]
        return far.at[pl.ds(unit, n)]

    for i in range(2):
        slab_wide[...] = slab_raw[i].astype(F32)
        for k in range(2):
            lanes = slice(k * LANES, (k + 1) * LANES)
            unit = join(slab_wide[:, 0, lanes], slab_wide[:, 1, lanes])
            slab(i, mine + flip(k, 2), 1)[...] = unit.astype(BF16)[None]

    build_taps(zh, taps_ref, line, wf, wa, rf, ra)

    def waves(t, ref):
        vy = ref[0:1, :]
        vx = ref[1:2, :]
        unit = lax.broadcasted_iota(jnp.int32, (16, LANES), 0)
        wide = lax.broadcasted_iota(jnp.int32, (3 * ROWS, LANES), 0)
        pos_r = ((r - 1) * ROWS + wide).astype(F32)
        pos_c = (flip(unit, 16) * LANES + lax.broadcasted_iota(jnp.int32, (16, LANES), 1)).astype(F32)
        turn_r = (vy * pos_r) * (1.0 / length)
        turn_c = (vx * pos_c) * (1.0 / length)
        ang_r = (2.0 * math.pi) * (turn_r - jnp.floor(turn_r + 0.5))
        ang_c = (2.0 * math.pi) * (turn_c - jnp.floor(turn_c + 0.5))
        cr, sr = jnp.cos(ang_r), jnp.sin(ang_r)
        cc, sc = jnp.cos(ang_c), jnp.sin(ang_c)
        for u in range(UNITS):
            re, im = times(cr, sr, cc[u : u + 1, :], sc[u : u + 1, :])
            inc[t, u, :, 0:LANES] = re
            inc[t, u, :, LANES:] = im

    waves(0, freq)
    for t in range(2):
        entry[t, 0] = jnp.zeros((3 * ROWS, 2 * LANES), BF16)
        entry[t, UNITS + 1] = jnp.zeros((3 * ROWS, 2 * LANES), BF16)
        field[t, 0] = jnp.zeros((ROWS, 2 * LANES), BF16)
        field[t, UNITS + 1] = jnp.zeros((ROWS, 2 * LANES), BF16)

    @pl.when(jnp.logical_not(has_up))
    def _():
        near[:, 0:ROWS, :] = jnp.zeros((UNITS, ROWS, 2 * LANES), BF16)
        halo[:, :, :, 0:ROWS, :] = jnp.zeros((3, 2, UNITS, ROWS, 2 * LANES), BF16)

    @pl.when(jnp.logical_not(has_dn))
    def _():
        near[:, 2 * ROWS :, :] = jnp.zeros((UNITS, ROWS, 2 * LANES), BF16)
        halo[:, :, :, 2 * ROWS :, :] = jnp.zeros((3, 2, UNITS, ROWS, 2 * LANES), BF16)

    for load in meas_loads:
        load.wait()

    beside = has_up.astype(jnp.int32) + has_dn.astype(jnp.int32)
    pl.semaphore_wait(barrier, 4 + beside * (1 + end.astype(jnp.int32)))

    def remote(src, dst, send_sem, recv_sem, to):
        return pltpu.make_async_remote_copy(
            src_ref=src,
            dst_ref=dst,
            send_sem=send_sem,
            recv_sem=recv_sem,
            device_id=to,
            device_id_type=MESH,
        )

    def slab_copy(i, k):
        block = slab(i, mine, 2)
        to = (r, 4 * zh + lax.rem(x + k, 4))
        return remote(block, block, slab_send.at[i, k - 1], slab_recv.at[i, k - 1], to)

    def slab_wait(i, k):
        block = slab(i, first_of(lax.rem(x + 4 - k, 4)), 2)
        remote(block, block, slab_send.at[i, k - 1], slab_recv.at[i, k - 1], (r, pair)).wait_recv()

    def edge_copy(i, d):
        lo = ROWS - ROWS * d
        dst = near.at[8:9, lo : lo + ROWS, :] if i == 0 else slab(1, 8, 1)
        row = (up, r, dn)[d + 1]
        sems = edge_send.at[i, d + 1], edge_recv.at[i, d + 1]
        return remote(slab(i, 7, 1), dst, *sems, (row, pair))

    def edge_each(sending, act):
        act(edge_copy(0, 0))
        act(edge_copy(1, 0))
        for d in (-1, 1):
            @pl.when(has_up if (d < 0) == sending else has_dn)
            def _():
                act(edge_copy(0, d))

    freq_copy = remote(freq, other_freq, freq_send, freq_recv, (r, pair))
    meas_copies = [
        remote(meas_from(1 - zh, u), meas_to(1, u), meas_send.at[u], meas_recv.at[u], (r, pair))
        for u in range(UNITS)
    ]

    def relay_copy(i, k):
        to = (r, 4 * zh + lax.rem(x + k, 4))
        margin = (near, far)[i].at[8]
        return remote(margin, margin, relay_send.at[i, k - 1], relay_recv.at[i], to)

    def margin_wait(i):
        @pl.when(jnp.logical_not(relay))
        def _():
            relay_copy(i, 1).wait_recv()

    def meas_start(*pieces):
        for u in pieces:
            meas_copies[u].start()

    freq_copy.start()

    @pl.when(owner)
    def _():
        edge_each(True, lambda copy: copy.start())

    for k in range(1, 4):
        slab_copy(0, k).start()

    @pl.when(jnp.logical_not(owner))
    def _():
        meas_start(*range(UNITS))

    for k in range(1, 4):
        slab_copy(1, k).start()

    def halo_copy(s, t, c, down):
        lo = 0 if down else 2 * ROWS
        i = 0 if down else 1
        u0, u1 = SLAB_PARTS[c] if s == 0 else PARTS[c]
        ref = near if s == 0 else halo.at[s - 1, t]
        return remote(
            ref.at[u0:u1, ROWS : 2 * ROWS, :],
            ref.at[u0:u1, lo : lo + ROWS, :],
            halo_send.at[s, t, c, i],
            halo_recv.at[s, t, c, i],
            (dn if down else up, a),
        )

    def halo_each(s, t, c, sending, act):
        @pl.when(has_dn if sending else has_up)
        def _():
            act(halo_copy(s, t, c, True))

        @pl.when(has_up if sending else has_dn)
        def _():
            act(halo_copy(s, t, c, False))

    def halo_start(s, t, c):
        halo_each(s, t, c, True, lambda copy: copy.start())

    def halo_wait(s, t, c):
        halo_each(s, t, c, False, lambda copy: copy.wait_recv())

    def halo_done(s, t, c):
        halo_each(s, t, c, True, lambda copy: copy.wait_send())

    def columns(ref, w, u0, u1):
        rows = ref.shape[1]
        acc = None
        for j in range(3):
            lhs = ref[u0 + j : u1 + j].reshape((u1 - u0) * rows, 2 * LANES)
            term = jnp.dot(lhs, w[j], preferred_element_type=F32)
            acc = term if acc is None else acc + term
        return acc.astype(BF16).reshape(u1 - u0, rows, 2 * LANES)

    def own(s, t, u0, u1, value):
        halo[s - 1, t, u0:u1, ROWS : 2 * ROWS, :] = value

    def enter(t):
        for u in range(UNITS):
            re, im = times(*parts(near[u]), *parts(inc[t, u]))
            entry[t, u + 1] = join(re, im).astype(BF16)
        for u0, u1 in PARTS:
            first[t, u0:u1] = columns(entry.at[t], wf, u0, u1)

    def second(t):
        for u in range(UNITS):
            re, im = row_correlate(rf, first[t, u])
            value = join(re, im).astype(BF16)
            inner[t, u] = value
            re, im = times(*parts(far[u]), *parts(value))
            field[t, u + 1] = join(re, im).astype(BF16)
        for c, (u0, u1) in enumerate(PARTS):
            own(1, t, u0, u1, columns(field.at[t], wf, u0, u1))
            halo_start(1, t, c)

    def compare(t, c):
        halo_wait(1, t, c)
        meas_wide[...] = meas_raw[t, c].astype(F32)
        for k in range(3):
            u = 3 * c + k
            re, im = row_correlate(rf, halo[0, t, u])
            value = join(re, im).astype(BF16)
            lanes = slice(k * LANES, (k + 1) * LANES)
            target = join(meas_wide[:, 0, lanes], meas_wide[:, 1, lanes])
            halo[1, t, u, ROWS : 2 * ROWS, :] = (value.astype(F32) - target).astype(BF16)
        halo_start(2, t, c)

    def back(s, t, c):
        halo_wait(s, t, c)
        for u in range(*PARTS[c]):
            re, im = row_correlate(ra, halo[s - 1, t, u])
            field[t, u + 1] = join(re, im).astype(BF16)

    def add(t, total, pack, u0, u1, re, im):
        grad = join(re, im)
        if t == 0:
            total[u0:u1] = grad
        else:
            grad = grad + total[u0:u1]
            total[u0:u1] = grad
            pack[u0:u1] = grad.astype(BF16)

    def back_far(t):
        def piece(c):
            u0, u1 = PARTS[c]
            br, bi = parts(columns(field.at[t], wa, u0, u1))
            re, im = conj_times(*parts(far[u0:u1]), br, bi)
            own(3, t, u0, u1, join(re, im).astype(BF16))
            halo_start(3, t, c)
            re, im = conj_times(*parts(inner[t, u0:u1]), br, bi)
            add(t, sum_far, pack_far, u0, u1, re, im)

        back(2, t, 0)
        back(2, t, 1)
        piece(0)
        back(2, t, 2)
        piece(1)
        piece(2)

    def back_near(t):
        def piece(c):
            u0, u1 = PARTS[c]
            br, bi = parts(columns(field.at[t], wa, u0, u1))
            re, im = conj_times(*parts(inc[t, u0:u1, ROWS : 2 * ROWS]), br, bi)
            add(t, sum_near, pack_near, u0, u1, re, im)

        back(3, t, 0)
        back(3, t, 1)
        piece(0)
        back(3, t, 2)
        piece(1)
        piece(2)

    grads = ((pack_near, got_near, sum_near), (pack_far, got_far, sum_far))

    def grad_copy(i, k):
        to = lax.rem(x + k, 4)
        src = grads[i][0].at[pl.ds(first_of(to), 2)]
        dst = grads[i][1].at[k - 1]
        return remote(src, dst, grad_send.at[i, k - 1], grad_recv.at[i, k - 1], (r, 4 * zh + to))

    def finish(i):
        _, got, total = grads[i]
        for k in range(1, 4):
            grad_copy(i, k).wait_recv()
        for j in range(2):
            at = flip(j, 2)
            value = total[mine + at]
            for k in range(3):
                value = value + got[k, at].astype(F32)
            out[i, :, 0, j * LANES : (j + 1) * LANES] = value[:, :LANES]
            out[i, :, 1, j * LANES : (j + 1) * LANES] = value[:, LANES:]

    for k in range(1, 4):
        slab_wait(0, k)
    halo_start(0, 0, 0)

    @pl.when(owner)
    def _():
        meas_start(*range(UNITS))

    @pl.when(relay)
    def _():
        edge_each(False, lambda copy: copy.wait_recv())
        for i in range(2):
            for k in range(1, 4):
                relay_copy(i, k).start()

    for k in range(1, 4):
        slab_wait(1, k)
    halo_wait(0, 0, 0)
    margin_wait(0)
    enter(0)
    freq_copy.wait_recv()
    waves(1, other_freq)
    enter(1)
    margin_wait(1)
    second(0)
    second(1)
    for c in range(3):
        compare(0, c)
    for c in range(3):
        for u in range(*PARTS[c]):
            meas_copies[u].wait_recv()
        compare(1, c)
    back_far(0)
    back_far(1)
    for k in range(1, 4):
        grad_copy(1, k).start()
    back_near(0)
    back_near(1)
    for k in range(1, 4):
        grad_copy(0, k).start()
    finish(1)
    finish(0)

    for i in range(2):
        for k in range(1, 4):
            slab_copy(i, k).wait_send()
            grad_copy(i, k).wait_send()

        @pl.when(owner)
        def _():
            if i == 0:
                edge_each(True, lambda copy: copy.wait_send())

        @pl.when(relay)
        def _():
            for k in range(1, 4):
                relay_copy(i, k).wait_send()

    freq_copy.wait_send()
    for copy in meas_copies:
        copy.wait_send()
    halo_done(0, 0, 0)
    for s in range(1, 4):
        for t in range(2):
            for c in range(3):
                halo_done(s, t, c)


def local(rows_n, measured, slices, kernel_taps, angle_freq, chosen):
    length = measured.shape[3]
    unit = (ROWS, 2 * LANES)
    wide = (3 * ROWS, 2 * LANES)
    vmem = pl.BlockSpec(memory_space=pltpu.VMEM)
    smem = pl.BlockSpec(memory_space=pltpu.SMEM)
    place = pl.BlockSpec(memory_space=pl.ANY)
    dma = pltpu.SemaphoreType.DMA
    grads = pl.pallas_call(
        functools.partial(kernel, rows_n, length),
        out_shape=jax.ShapeDtypeStruct((2, ROWS, 2, 2 * LANES), F32),
        in_specs=[smem, smem, vmem, place, place],
        out_specs=vmem,
        scratch_shapes=[
            pltpu.VMEM((2, ROWS, 2, 2 * LANES), BF16),
            pltpu.VMEM((ROWS, 2, 2 * LANES), F32),
            pltpu.VMEM((2, 3, ROWS, 2, PIECE), BF16),
            pltpu.VMEM((ROWS, 2, PIECE), F32),
            pltpu.VMEM((UNITS,) + wide, BF16),
            pltpu.VMEM((UNITS,) + unit, BF16),
            pltpu.VMEM((2, LANES), F32),
            pltpu.VMEM((2, LANES), F32),
            pltpu.VMEM((8, 4 * LANES), F32),
            pltpu.VMEM((3, 2 * LANES, 2 * LANES), BF16),
            pltpu.VMEM((3, 2 * LANES, 2 * LANES), BF16),
            pltpu.VMEM((2 * ROWS, LANES), BF16),
            pltpu.VMEM((2 * ROWS, LANES), BF16),
            pltpu.VMEM((2, UNITS) + wide, F32),
            pltpu.VMEM((2, UNITS) + unit, BF16),
            pltpu.VMEM((2, UNITS + 2) + wide, BF16),
            pltpu.VMEM((2, UNITS) + wide, BF16),
            pltpu.VMEM((2, UNITS + 2) + unit, BF16),
            pltpu.VMEM((3, 2, UNITS) + wide, BF16),
            pltpu.VMEM((UNITS,) + unit, F32),
            pltpu.VMEM((UNITS,) + unit, F32),
            pltpu.VMEM((UNITS,) + unit, BF16),
            pltpu.VMEM((UNITS,) + unit, BF16),
            pltpu.VMEM((3, 2) + unit, BF16),
            pltpu.VMEM((3, 2) + unit, BF16),
            dma((1 + UNITS,)),
            dma((2, 3)),
            dma((2, 3)),
            dma((2, 3)),
            dma((2, 3)),
            dma((2, 3)),
            dma((2,)),
            dma,
            dma,
            dma((UNITS,)),
            dma((UNITS,)),
            dma((4, 2, 3, 2)),
            dma((4, 2, 3, 2)),
            dma((2, 3)),
            dma((2, 3)),
        ],
        compiler_params=pltpu.CompilerParams(collective_id=0, has_side_effects=True),
    )(chosen, angle_freq.T, kernel_taps, slices, measured)
    return grads[0], grads[1]


def solution(mesh):
    return jax.shard_map(
        functools.partial(local, mesh.shape["rows"]),
        mesh=mesh,
        in_specs=(P("ang", "rows", None, None), P(None, "rows", None, "ang"), P(), P(), P("ang")),
        out_specs=(P("rows", None, "ang"), P("rows", None, "ang")),
        check_vma=False,
    )
```

```python
import functools
import math

import jax
import jax.numpy as jnp
from jax import lax
from jax.experimental import pallas as pl
from jax.experimental.pallas import tpu as pltpu
from jax.sharding import PartitionSpec as P

MESH = pl.DeviceIdType.MESH
F32 = jnp.float32
BF16 = jnp.bfloat16
ROWS = 32
LANES = 128
UNITS = 9
REACH = 32
TAPS = 65


def build_taps(zh, taps_ref, line, wf, wa, rf, ra):
    line[...] = jnp.zeros_like(line)
    line[0:2, 0:TAPS] = taps_ref[...].astype(F32)
    gr = line[0:1, :]
    gi = line[1:2, :]

    def column(vec, j):
        wide = jnp.broadcast_to(vec, (LANES, 4 * LANES))
        shift = (LANES * (j - 1) - REACH) % (4 * LANES)
        return pltpu.roll(wide, shift, 1, stride=1, stride_axis=0)[:, :LANES]

    for j in range(3):
        re = column(gr, j)
        im = column(gi, j)
        ja = j + zh * (2 - 2 * j)
        jf = 2 - ja
        wa[ja, 0:LANES, 0:LANES] = re.astype(BF16)
        wa[ja, 0:LANES, LANES:] = (-im).astype(BF16)
        wa[ja, LANES:, 0:LANES] = im.astype(BF16)
        wa[ja, LANES:, LANES:] = re.astype(BF16)
        ret = re.T
        imt = im.T
        wf[jf, 0:LANES, 0:LANES] = ret.astype(BF16)
        wf[jf, 0:LANES, LANES:] = imt.astype(BF16)
        wf[jf, LANES:, 0:LANES] = (-imt).astype(BF16)
        wf[jf, LANES:, LANES:] = ret.astype(BF16)

    def row(vec, sign):
        narrow = vec[:, :LANES]
        ahead = pltpu.roll(jnp.broadcast_to(narrow, (ROWS, LANES)), 0, 1, stride=1, stride_axis=0)
        back = pltpu.roll(
            jnp.broadcast_to(narrow, (LANES, LANES)), LANES - 2 * REACH, 1, stride=1, stride_axis=0
        )
        return ahead, sign * back.T[0:ROWS, :]

    fr, br = row(gr, 1.0)
    fi, bi = row(gi, -1.0)
    rf[0:ROWS, :] = fr.astype(BF16)
    rf[ROWS:, :] = fi.astype(BF16)
    ra[0:ROWS, :] = br.astype(BF16)
    ra[ROWS:, :] = bi.astype(BF16)


def row_correlate(taps, window):
    both = jnp.dot(taps[:, 0 : 3 * ROWS], window, preferred_element_type=F32)
    re = both[:ROWS, :LANES] - both[ROWS:, LANES:]
    im = both[:ROWS, LANES:] + both[ROWS:, :LANES]
    return re, im


def times(ar, ai, br, bi):
    return ar * br - ai * bi, ar * bi + ai * br


def conj_times(ar, ai, br, bi):
    return ar * br + ai * bi, ar * bi - ai * br


def join(re, im):
    return jnp.concatenate([re, im], axis=-1)


def parts(value):
    value = value.astype(F32)
    return value[..., :LANES], value[..., LANES:]


SLAB_PARTS = ((0, 4), (4, 8))
PARTS = ((0, 3), (3, 6), (6, 9))
PIECE = 3 * LANES


def kernel(
    rows_n,
    length,
    chosen_ref,
    table_ref,
    taps_ref,
    slices_ref,
    meas_ref,
    out,
    slab_raw,
    slab_wide,
    meas_raw,
    meas_wide,
    near,
    far,
    freq,
    other_freq,
    line,
    wf,
    wa,
    rf,
    ra,
    inc,
    inner,
    entry,
    first,
    field,
    halo,
    sum_near,
    sum_far,
    pack_near,
    pack_far,
    got_near,
    got_far,
    result,
    load_sem,
    slab_send,
    slab_recv,
    edge_send,
    edge_recv,
    relay_send,
    relay_recv,
    freq_send,
    freq_recv,
    meas_send,
    meas_recv,
    halo_send,
    halo_recv,
    grad_send,
    grad_recv,
):
    r = lax.axis_index("rows")
    a = lax.axis_index("ang")
    zh = a // 4
    x = lax.rem(a, 4)
    has_up = r > 0
    has_dn = r < rows_n - 1
    up = lax.rem(r + rows_n - 1, rows_n)
    dn = lax.rem(r + 1, rows_n)
    pair = lax.rem(a + 4, 8)

    def first_of(other_x):
        return 2 * other_x + zh * (6 - 4 * other_x)

    mine = first_of(x)

    def flip(i, n):
        return i + zh * (n - 1 - 2 * i)

    barrier = pltpu.get_barrier_semaphore()
    pl.semaphore_signal(barrier, inc=1, device_id=(r, pair), device_id_type=MESH)
    for k in range(1, 4):
        to = (r, 4 * zh + lax.rem(x + k, 4))
        pl.semaphore_signal(barrier, inc=1, device_id=to, device_id_type=MESH)

    owner = mine == 6
    relay = mine == 0
    end = jnp.logical_or(owner, relay)
    for has, row in ((has_up, up), (has_dn, dn)):

        @pl.when(has)
        def _():
            pl.semaphore_signal(barrier, inc=1, device_id=(row, a), device_id_type=MESH)

        @pl.when(jnp.logical_and(has, end))
        def _():
            pl.semaphore_signal(barrier, inc=1, device_id=(row, pair), device_id_type=MESH)

    def meas_from(half):
        return meas_ref.at[0, :, :, pl.ds(pl.multiple_of(7 * half * LANES, LANES), UNITS * LANES)]

    slab_load = pltpu.make_async_copy(slices_ref, slab_raw, load_sem.at[0])
    slab_load.start()
    meas_load = pltpu.make_async_copy(meas_from(zh), meas_raw.at[0], load_sem.at[1])
    meas_load.start()

    fy = table_ref[0, chosen_ref[0]]
    fx = table_ref[1, chosen_ref[0]]
    freq[0:1, :] = jnp.full((1, LANES), fy, F32)
    freq[1:2, :] = jnp.full((1, LANES), fx, F32)

    slab_load.wait()

    def slab(i, unit, n):
        if i == 0:
            return near.at[pl.ds(unit, n), ROWS : 2 * ROWS, :]
        return far.at[pl.ds(unit, n)]

    for i in range(2):
        slab_wide[...] = slab_raw[i].astype(F32)
        for k in range(2):
            lanes = slice(k * LANES, (k + 1) * LANES)
            unit = join(slab_wide[:, 0, lanes], slab_wide[:, 1, lanes])
            slab(i, mine + flip(k, 2), 1)[...] = unit.astype(BF16)[None]

    build_taps(zh, taps_ref, line, wf, wa, rf, ra)

    def waves(t, ref):
        vy = ref[0:1, :]
        vx = ref[1:2, :]
        unit = lax.broadcasted_iota(jnp.int32, (16, LANES), 0)
        wide = lax.broadcasted_iota(jnp.int32, (3 * ROWS, LANES), 0)
        pos_r = ((r - 1) * ROWS + wide).astype(F32)
        pos_c = (flip(unit, 16) * LANES + lax.broadcasted_iota(jnp.int32, (16, LANES), 1)).astype(F32)
        turn_r = (vy * pos_r) * (1.0 / length)
        turn_c = (vx * pos_c) * (1.0 / length)
        ang_r = (2.0 * math.pi) * (turn_r - jnp.floor(turn_r + 0.5))
        ang_c = (2.0 * math.pi) * (turn_c - jnp.floor(turn_c + 0.5))
        cr, sr = jnp.cos(ang_r), jnp.sin(ang_r)
        cc, sc = jnp.cos(ang_c), jnp.sin(ang_c)
        for u in range(UNITS):
            re, im = times(cr, sr, cc[u : u + 1, :], sc[u : u + 1, :])
            inc[t, u, :, 0:LANES] = re
            inc[t, u, :, LANES:] = im

    @pl.when(jnp.logical_not(has_up))
    def _():
        near[:, 0:ROWS, :] = jnp.zeros((UNITS, ROWS, 2 * LANES), BF16)
        halo[:, :, :, 0:ROWS, :] = jnp.zeros((3, 2, UNITS, ROWS, 2 * LANES), BF16)

    @pl.when(jnp.logical_not(has_dn))
    def _():
        near[:, 2 * ROWS :, :] = jnp.zeros((UNITS, ROWS, 2 * LANES), BF16)
        halo[:, :, :, 2 * ROWS :, :] = jnp.zeros((3, 2, UNITS, ROWS, 2 * LANES), BF16)

    beside = has_up.astype(jnp.int32) + has_dn.astype(jnp.int32)
    pl.semaphore_wait(barrier, 4 + beside * (1 + end.astype(jnp.int32)))

    def remote(src, dst, send_sem, recv_sem, to):
        return pltpu.make_async_remote_copy(
            src_ref=src,
            dst_ref=dst,
            send_sem=send_sem,
            recv_sem=recv_sem,
            device_id=to,
            device_id_type=MESH,
        )

    def slab_copy(i, k):
        block = slab(i, mine, 2)
        to = (r, 4 * zh + lax.rem(x + k, 4))
        return remote(block, block, slab_send.at[i, k - 1], slab_recv.at[i, k - 1], to)

    def slab_wait(i, k):
        block = slab(i, first_of(lax.rem(x + 4 - k, 4)), 2)
        remote(block, block, slab_send.at[i, k - 1], slab_recv.at[i, k - 1], (r, pair)).wait_recv()

    def edge_copy(i, d):
        lo = ROWS - ROWS * d
        dst = near.at[8:9, lo : lo + ROWS, :] if i == 0 else slab(1, 8, 1)
        row = (up, r, dn)[d + 1]
        sems = edge_send.at[i, d + 1], edge_recv.at[i, d + 1]
        return remote(slab(i, 7, 1), dst, *sems, (row, pair))

    def edge_each(sending, act):
        act(edge_copy(0, 0))
        act(edge_copy(1, 0))
        for d in (-1, 1):
            @pl.when(has_up if (d < 0) == sending else has_dn)
            def _():
                act(edge_copy(0, d))

    freq_copy = remote(freq, other_freq, freq_send, freq_recv, (r, pair))
    def meas_copy(c):
        half = 1 - zh
        at = (c + half * (2 - 2 * c)) * PIECE
        lanes = pl.ds(pl.multiple_of(at, LANES), PIECE)
        start = pl.multiple_of(7 * half * LANES + at, LANES)
        src = meas_ref.at[0, :, :, pl.ds(start, PIECE)]
        dst = meas_raw.at[1, :, :, lanes]
        return remote(src, dst, meas_send.at[c], meas_recv.at[c], (r, pair))

    def meas_wait(c):
        lanes = pl.ds(pl.multiple_of(flip(c, 3) * PIECE, LANES), PIECE)
        dst = meas_raw.at[1, :, :, lanes]
        remote(dst, dst, meas_send.at[c], meas_recv.at[c], (r, pair)).wait_recv()


    def relay_copy(i, k):
        to = (r, 4 * zh + lax.rem(x + k, 4))
        margin = (near, far)[i].at[8]
        return remote(margin, margin, relay_send.at[i, k - 1], relay_recv.at[i], to)

    def margin_wait(i):
        @pl.when(jnp.logical_not(relay))
        def _():
            relay_copy(i, 1).wait_recv()

    freq_copy.start()

    @pl.when(owner)
    def _():
        edge_each(True, lambda copy: copy.start())

    for k in range(1, 4):
        slab_copy(0, k).start()

    @pl.when(jnp.logical_not(owner))
    def _():
        for c in range(3):
            meas_copy(c).start()

    for k in range(1, 4):
        slab_copy(1, k).start()

    def halo_copy(s, t, c, down):
        lo = 0 if down else 2 * ROWS
        i = 0 if down else 1
        u0, u1 = SLAB_PARTS[c] if s == 0 else PARTS[c]
        ref = near if s == 0 else halo.at[s - 1, t]
        return remote(
            ref.at[u0:u1, ROWS : 2 * ROWS, :],
            ref.at[u0:u1, lo : lo + ROWS, :],
            halo_send.at[s, t, c, i],
            halo_recv.at[s, t, c, i],
            (dn if down else up, a),
        )

    def halo_each(s, t, c, sending, act):
        @pl.when(has_dn if sending else has_up)
        def _():
            act(halo_copy(s, t, c, True))

        @pl.when(has_up if sending else has_dn)
        def _():
            act(halo_copy(s, t, c, False))

    def halo_start(s, t, c):
        halo_each(s, t, c, True, lambda copy: copy.start())

    def halo_wait(s, t, c):
        halo_each(s, t, c, False, lambda copy: copy.wait_recv())

    def halo_done(s, t, c):
        halo_each(s, t, c, True, lambda copy: copy.wait_send())

    def columns(ref, w, u0, u1):
        rows = ref.shape[1]
        acc = None
        for j in range(3):
            lhs = ref[u0 + j : u1 + j].reshape((u1 - u0) * rows, 2 * LANES)
            term = jnp.dot(lhs, w[j], preferred_element_type=F32)
            acc = term if acc is None else acc + term
        return acc.astype(BF16).reshape(u1 - u0, rows, 2 * LANES)

    def own(s, t, u0, u1, value):
        halo[s - 1, t, u0:u1, ROWS : 2 * ROWS, :] = value

    def enter(t):
        at = 0
        for c, (u0, u1) in enumerate(PARTS):
            if t == 0:
                if c < 2:
                    halo_wait(0, 0, c)
                else:
                    margin_wait(0)
            ahead = min(u1 + 1, UNITS)
            for u in range(at, ahead):
                re, im = times(*parts(near[u]), *parts(inc[t, u]))
                entry[t, u + 1] = join(re, im).astype(BF16)
            at = ahead
            first[t, u0:u1] = columns(entry.at[t], wf, u0, u1)

    def second(t):
        for u in range(UNITS):
            re, im = row_correlate(rf, first[t, u])
            value = join(re, im).astype(BF16)
            inner[t, u] = value
            re, im = times(*parts(far[u]), *parts(value))
            field[t, u + 1] = join(re, im).astype(BF16)
        for c, (u0, u1) in enumerate(PARTS):
            own(1, t, u0, u1, columns(field.at[t], wf, u0, u1))
            halo_start(1, t, c)

    def compare(t, c):
        halo_wait(1, t, c)
        lanes = pl.ds(pl.multiple_of(flip(c, 3) * PIECE, LANES), PIECE)
        meas_wide[...] = meas_raw[t, :, :, lanes].astype(F32)
        for k in range(3):
            u = 3 * c + k
            re, im = row_correlate(rf, halo[0, t, u])
            value = join(re, im).astype(BF16)
            lanes = pl.ds(pl.multiple_of(flip(k, 3) * LANES, LANES), LANES)
            target = join(meas_wide[:, 0, lanes], meas_wide[:, 1, lanes])
            halo[1, t, u, ROWS : 2 * ROWS, :] = (value.astype(F32) - target).astype(BF16)
        halo_start(2, t, c)

    def back(s, t, c):
        halo_wait(s, t, c)
        for u in range(*PARTS[c]):
            re, im = row_correlate(ra, halo[s - 1, t, u])
            field[t, u + 1] = join(re, im).astype(BF16)

    def add(t, total, pack, u0, u1, re, im):
        grad = join(re, im)
        if t == 0:
            total[u0:u1] = grad
        else:
            grad = grad + total[u0:u1]
            total[u0:u1] = grad
            pack[u0:u1] = grad.astype(BF16)

    def back_far(t):
        def piece(c):
            u0, u1 = PARTS[c]
            br, bi = parts(columns(field.at[t], wa, u0, u1))
            re, im = conj_times(*parts(far[u0:u1]), br, bi)
            own(3, t, u0, u1, join(re, im).astype(BF16))
            halo_start(3, t, c)
            re, im = conj_times(*parts(inner[t, u0:u1]), br, bi)
            add(t, sum_far, pack_far, u0, u1, re, im)

        back(2, t, 0)
        back(2, t, 1)
        piece(0)
        back(2, t, 2)
        piece(1)
        piece(2)

    def back_near(t):
        def piece(c):
            u0, u1 = PARTS[c]
            br, bi = parts(columns(field.at[t], wa, u0, u1))
            re, im = conj_times(*parts(inc[t, u0:u1, ROWS : 2 * ROWS]), br, bi)
            add(t, sum_near, pack_near, u0, u1, re, im)

        back(3, t, 0)
        back(3, t, 1)
        piece(0)
        back(3, t, 2)
        piece(1)
        piece(2)

    grads = ((pack_near, got_near, sum_near), (pack_far, got_far, sum_far))

    def grad_copy(i, k):
        to = lax.rem(x + k, 4)
        src = grads[i][0].at[pl.ds(first_of(to), 2)]
        dst = grads[i][1].at[k - 1]
        return remote(src, dst, grad_send.at[i, k - 1], grad_recv.at[i, k - 1], (r, 4 * zh + to))

    def finish(i):
        _, got, total = grads[i]
        for k in range(1, 4):
            grad_copy(i, k).wait_recv()
        for j in range(2):
            at = flip(j, 2)
            value = total[mine + at]
            for k in range(3):
                value = value + got[k, at].astype(F32)
            result[i, :, 0, j * LANES : (j + 1) * LANES] = value[:, :LANES]
            result[i, :, 1, j * LANES : (j + 1) * LANES] = value[:, LANES:]

    waves(0, freq)
    for t in range(2):
        entry[t, 0] = jnp.zeros((3 * ROWS, 2 * LANES), BF16)
        entry[t, UNITS + 1] = jnp.zeros((3 * ROWS, 2 * LANES), BF16)
        field[t, 0] = jnp.zeros((ROWS, 2 * LANES), BF16)
        field[t, UNITS + 1] = jnp.zeros((ROWS, 2 * LANES), BF16)

    for k in range(1, 4):
        slab_wait(0, k)
    halo_start(0, 0, 0)
    halo_start(0, 0, 1)

    @pl.when(owner)
    def _():
        for c in range(3):
            meas_copy(c).start()

    @pl.when(relay)
    def _():
        edge_each(False, lambda copy: copy.wait_recv())
        for i in range(2):
            for k in range(1, 4):
                relay_copy(i, k).start()

    for k in range(1, 4):
        slab_wait(1, k)
    enter(0)
    freq_copy.wait_recv()
    waves(1, other_freq)
    enter(1)
    meas_load.wait()
    margin_wait(1)
    second(0)
    second(1)
    for c in range(3):
        compare(0, c)
    for c in range(3):
        meas_wait(c)
        compare(1, c)
    back_far(0)
    back_far(1)
    for k in range(1, 4):
        grad_copy(1, k).start()
    back_near(0)
    back_near(1)
    for k in range(1, 4):
        grad_copy(0, k).start()
    stores = [pltpu.make_async_copy(result.at[i], out.at[i], load_sem.at[2 + i]) for i in range(2)]
    finish(1)
    stores[1].start()
    finish(0)
    stores[0].start()

    for i in range(2):
        for k in range(1, 4):
            slab_copy(i, k).wait_send()
            grad_copy(i, k).wait_send()

        @pl.when(owner)
        def _():
            if i == 0:
                edge_each(True, lambda copy: copy.wait_send())

        @pl.when(relay)
        def _():
            for k in range(1, 4):
                relay_copy(i, k).wait_send()

    freq_copy.wait_send()
    for c in range(3):
        meas_copy(c).wait_send()
    for store in stores:
        store.wait()
    halo_done(0, 0, 0)
    halo_done(0, 0, 1)
    for s in range(1, 4):
        for t in range(2):
            for c in range(3):
                halo_done(s, t, c)


def local(rows_n, measured, slices, kernel_taps, angle_freq, chosen):
    length = measured.shape[3]
    unit = (ROWS, 2 * LANES)
    wide = (3 * ROWS, 2 * LANES)
    vmem = pl.BlockSpec(memory_space=pltpu.VMEM)
    smem = pl.BlockSpec(memory_space=pltpu.SMEM)
    hbm = pl.BlockSpec(memory_space=pltpu.HBM)
    dma = pltpu.SemaphoreType.DMA
    grads = pl.pallas_call(
        functools.partial(kernel, rows_n, length),
        out_shape=jax.ShapeDtypeStruct((2, ROWS, 2, 2 * LANES), F32),
        in_specs=[smem, smem, vmem, hbm, hbm],
        out_specs=pl.BlockSpec(memory_space=pl.ANY),
        scratch_shapes=[
            pltpu.VMEM((2, ROWS, 2, 2 * LANES), BF16),
            pltpu.VMEM((ROWS, 2, 2 * LANES), F32),
            pltpu.VMEM((2, ROWS, 2, UNITS * LANES), BF16),
            pltpu.VMEM((ROWS, 2, PIECE), F32),
            pltpu.VMEM((UNITS,) + wide, BF16),
            pltpu.VMEM((UNITS,) + unit, BF16),
            pltpu.VMEM((2, LANES), F32),
            pltpu.VMEM((2, LANES), F32),
            pltpu.VMEM((8, 4 * LANES), F32),
            pltpu.VMEM((3, 2 * LANES, 2 * LANES), BF16),
            pltpu.VMEM((3, 2 * LANES, 2 * LANES), BF16),
            pltpu.VMEM((2 * ROWS, LANES), BF16),
            pltpu.VMEM((2 * ROWS, LANES), BF16),
            pltpu.VMEM((2, UNITS) + wide, F32),
            pltpu.VMEM((2, UNITS) + unit, BF16),
            pltpu.VMEM((2, UNITS + 2) + wide, BF16),
            pltpu.VMEM((2, UNITS) + wide, BF16),
            pltpu.VMEM((2, UNITS + 2) + unit, BF16),
            pltpu.VMEM((3, 2, UNITS) + wide, BF16),
            pltpu.VMEM((UNITS,) + unit, F32),
            pltpu.VMEM((UNITS,) + unit, F32),
            pltpu.VMEM((UNITS,) + unit, BF16),
            pltpu.VMEM((UNITS,) + unit, BF16),
            pltpu.VMEM((3, 2) + unit, BF16),
            pltpu.VMEM((3, 2) + unit, BF16),
            pltpu.VMEM((2, ROWS, 2, 2 * LANES), F32),
            dma((4,)),
            dma((2, 3)),
            dma((2, 3)),
            dma((2, 3)),
            dma((2, 3)),
            dma((2, 3)),
            dma((2,)),
            dma,
            dma,
            dma((3,)),
            dma((3,)),
            dma((4, 2, 3, 2)),
            dma((4, 2, 3, 2)),
            dma((2, 3)),
            dma((2, 3)),
        ],
        compiler_params=pltpu.CompilerParams(
            collective_id=0, has_side_effects=True, vmem_limit_bytes=24 * 2**20
        ),
    )(
        chosen,
        angle_freq.T,
        kernel_taps,
        pltpu.with_memory_space_constraint(slices, pltpu.HBM),
        pltpu.with_memory_space_constraint(measured, pltpu.HBM),
    )
    return grads[0], grads[1]


def solution(mesh):
    return jax.shard_map(
        functools.partial(local, mesh.shape["rows"]),
        mesh=mesh,
        in_specs=(P("ang", "rows", None, None), P(None, "rows", None, "ang"), P(), P(), P("ang")),
        out_specs=(P("rows", None, "ang"), P("rows", None, "ang")),
        check_vma=False,
    )
```

```python
import functools
import math

import jax
import jax.numpy as jnp
from jax import lax
from jax.experimental import pallas as pl
from jax.experimental.pallas import tpu as pltpu
from jax.sharding import PartitionSpec as P

MESH = pl.DeviceIdType.MESH
F32 = jnp.float32
BF16 = jnp.bfloat16
ROWS = 32
LANES = 128
UNITS = 9
REACH = 32
TAPS = 65


def build_taps(zh, taps_ref, line, wf, wa, rf, ra):
    line[...] = jnp.zeros_like(line)
    line[0:2, 0:TAPS] = taps_ref[...].astype(F32)
    gr = line[0:1, :]
    gi = line[1:2, :]

    def column(vec, j):
        wide = jnp.broadcast_to(vec, (LANES, 4 * LANES))
        shift = (LANES * (j - 1) - REACH) % (4 * LANES)
        return pltpu.roll(wide, shift, 1, stride=1, stride_axis=0)[:, :LANES]

    for j in range(3):
        re = column(gr, j)
        im = column(gi, j)
        ja = j + zh * (2 - 2 * j)
        jf = 2 - ja
        wa[ja, 0:LANES, 0:LANES] = re.astype(BF16)
        wa[ja, 0:LANES, LANES:] = (-im).astype(BF16)
        wa[ja, LANES:, 0:LANES] = im.astype(BF16)
        wa[ja, LANES:, LANES:] = re.astype(BF16)
        ret = re.T
        imt = im.T
        wf[jf, 0:LANES, 0:LANES] = ret.astype(BF16)
        wf[jf, 0:LANES, LANES:] = imt.astype(BF16)
        wf[jf, LANES:, 0:LANES] = (-imt).astype(BF16)
        wf[jf, LANES:, LANES:] = ret.astype(BF16)

    def row(vec, sign):
        narrow = vec[:, :LANES]
        ahead = pltpu.roll(jnp.broadcast_to(narrow, (ROWS, LANES)), 0, 1, stride=1, stride_axis=0)
        back = pltpu.roll(
            jnp.broadcast_to(narrow, (LANES, LANES)), LANES - 2 * REACH, 1, stride=1, stride_axis=0
        )
        return ahead, sign * back.T[0:ROWS, :]

    fr, br = row(gr, 1.0)
    fi, bi = row(gi, -1.0)
    rf[0:ROWS, :] = fr.astype(BF16)
    rf[ROWS:, :] = fi.astype(BF16)
    ra[0:ROWS, :] = br.astype(BF16)
    ra[ROWS:, :] = bi.astype(BF16)


def row_correlate(taps, window):
    both = jnp.dot(taps[:, 0 : 3 * ROWS], window, preferred_element_type=F32)
    re = both[:ROWS, :LANES] - both[ROWS:, LANES:]
    im = both[:ROWS, LANES:] + both[ROWS:, :LANES]
    return re, im


def times(ar, ai, br, bi):
    return ar * br - ai * bi, ar * bi + ai * br


def conj_times(ar, ai, br, bi):
    return ar * br + ai * bi, ar * bi - ai * br


def join(re, im):
    return jnp.concatenate([re, im], axis=-1)


def parts(value):
    value = value.astype(F32)
    return value[..., :LANES], value[..., LANES:]


SLAB_PARTS = ((0, 4), (4, 8))
PARTS = ((0, 3), (3, 6), (6, 9))
PIECE = 3 * LANES


def kernel(
    rows_n,
    length,
    chosen_ref,
    table_ref,
    taps_ref,
    slices_ref,
    meas_ref,
    out,
    slab_raw,
    slab_wide,
    meas_raw,
    meas_wide,
    near,
    far,
    freq,
    other_freq,
    line,
    wf,
    wa,
    rf,
    ra,
    inc,
    inner,
    entry,
    first,
    field,
    halo,
    sum_near,
    sum_far,
    pack_near,
    pack_far,
    got_near,
    got_far,
    result,
    load_sem,
    slab_send,
    slab_recv,
    edge_send,
    edge_recv,
    relay_send,
    relay_recv,
    freq_send,
    freq_recv,
    meas_send,
    meas_recv,
    halo_send,
    halo_recv,
    grad_send,
    grad_recv,
):
    r = lax.axis_index("rows")
    a = lax.axis_index("ang")
    zh = a // 4
    x = lax.rem(a, 4)
    has_up = r > 0
    has_dn = r < rows_n - 1
    up = lax.rem(r + rows_n - 1, rows_n)
    dn = lax.rem(r + 1, rows_n)
    pair = lax.rem(a + 4, 8)

    def first_of(other_x):
        return 2 * other_x + zh * (6 - 4 * other_x)

    mine = first_of(x)

    def flip(i, n):
        return i + zh * (n - 1 - 2 * i)

    barrier = pltpu.get_barrier_semaphore()
    pl.semaphore_signal(barrier, inc=1, device_id=(r, pair), device_id_type=MESH)
    for k in range(1, 4):
        to = (r, 4 * zh + lax.rem(x + k, 4))
        pl.semaphore_signal(barrier, inc=1, device_id=to, device_id_type=MESH)

    owner = mine == 6
    relay = mine == 0
    end = jnp.logical_or(owner, relay)
    for has, row in ((has_up, up), (has_dn, dn)):

        @pl.when(has)
        def _():
            pl.semaphore_signal(barrier, inc=1, device_id=(row, a), device_id_type=MESH)

        @pl.when(jnp.logical_and(has, end))
        def _():
            pl.semaphore_signal(barrier, inc=1, device_id=(row, pair), device_id_type=MESH)

    def meas_from(half):
        return meas_ref.at[0, :, :, pl.ds(pl.multiple_of(7 * half * LANES, LANES), UNITS * LANES)]

    slab_load = pltpu.make_async_copy(slices_ref, slab_raw, load_sem.at[0])
    slab_load.start()
    meas_load = pltpu.make_async_copy(meas_from(zh), meas_raw.at[0], load_sem.at[1])
    meas_load.start()

    fy = table_ref[0, chosen_ref[0]]
    fx = table_ref[1, chosen_ref[0]]
    freq[0:1, :] = jnp.full((1, LANES), fy, F32)
    freq[1:2, :] = jnp.full((1, LANES), fx, F32)

    slab_load.wait()

    def slab(i, unit, n):
        if i == 0:
            return near.at[pl.ds(unit, n), ROWS : 2 * ROWS, :]
        return far.at[pl.ds(unit, n)]

    for i in range(2):
        slab_wide[...] = slab_raw[i].astype(F32)
        for k in range(2):
            lanes = slice(k * LANES, (k + 1) * LANES)
            unit = join(slab_wide[:, 0, lanes], slab_wide[:, 1, lanes])
            slab(i, mine + flip(k, 2), 1)[...] = unit.astype(BF16)[None]

    build_taps(zh, taps_ref, line, wf, wa, rf, ra)

    def waves(t, ref):
        vy = ref[0:1, :]
        vx = ref[1:2, :]
        unit = lax.broadcasted_iota(jnp.int32, (16, LANES), 0)
        wide = lax.broadcasted_iota(jnp.int32, (3 * ROWS, LANES), 0)
        pos_r = ((r - 1) * ROWS + wide).astype(F32)
        pos_c = (flip(unit, 16) * LANES + lax.broadcasted_iota(jnp.int32, (16, LANES), 1)).astype(F32)
        turn_r = (vy * pos_r) * (1.0 / length)
        turn_c = (vx * pos_c) * (1.0 / length)
        ang_r = (2.0 * math.pi) * (turn_r - jnp.floor(turn_r + 0.5))
        ang_c = (2.0 * math.pi) * (turn_c - jnp.floor(turn_c + 0.5))
        cr, sr = jnp.cos(ang_r), jnp.sin(ang_r)
        cc, sc = jnp.cos(ang_c), jnp.sin(ang_c)
        for u in range(UNITS):
            re, im = times(cr, sr, cc[u : u + 1, :], sc[u : u + 1, :])
            inc[t, u, :, 0:LANES] = re
            inc[t, u, :, LANES:] = im

    @pl.when(jnp.logical_not(has_up))
    def _():
        near[:, 0:ROWS, :] = jnp.zeros((UNITS, ROWS, 2 * LANES), BF16)
        halo[:, :, :, 0:ROWS, :] = jnp.zeros((3, 2, UNITS, ROWS, 2 * LANES), BF16)

    @pl.when(jnp.logical_not(has_dn))
    def _():
        near[:, 2 * ROWS :, :] = jnp.zeros((UNITS, ROWS, 2 * LANES), BF16)
        halo[:, :, :, 2 * ROWS :, :] = jnp.zeros((3, 2, UNITS, ROWS, 2 * LANES), BF16)

    beside = has_up.astype(jnp.int32) + has_dn.astype(jnp.int32)
    pl.semaphore_wait(barrier, 4 + beside * (1 + end.astype(jnp.int32)))

    def remote(src, dst, send_sem, recv_sem, to):
        return pltpu.make_async_remote_copy(
            src_ref=src,
            dst_ref=dst,
            send_sem=send_sem,
            recv_sem=recv_sem,
            device_id=to,
            device_id_type=MESH,
        )

    def slab_copy(i, k):
        block = slab(i, mine, 2)
        to = (r, 4 * zh + lax.rem(x + k, 4))
        return remote(block, block, slab_send.at[i, k - 1], slab_recv.at[i, k - 1], to)

    def slab_wait(i, k):
        block = slab(i, first_of(lax.rem(x + 4 - k, 4)), 2)
        remote(block, block, slab_send.at[i, k - 1], slab_recv.at[i, k - 1], (r, pair)).wait_recv()

    def edge_copy(i, d):
        lo = ROWS - ROWS * d
        dst = near.at[8:9, lo : lo + ROWS, :] if i == 0 else slab(1, 8, 1)
        row = (up, r, dn)[d + 1]
        sems = edge_send.at[i, d + 1], edge_recv.at[i, d + 1]
        return remote(slab(i, 7, 1), dst, *sems, (row, pair))

    def edge_each(sending, act):
        act(edge_copy(0, 0))
        act(edge_copy(1, 0))
        for d in (-1, 1):
            @pl.when(has_up if (d < 0) == sending else has_dn)
            def _():
                act(edge_copy(0, d))

    freq_copy = remote(freq, other_freq, freq_send, freq_recv, (r, pair))
    def meas_copy(c):
        half = 1 - zh
        at = (c + half * (2 - 2 * c)) * PIECE
        lanes = pl.ds(pl.multiple_of(at, LANES), PIECE)
        start = pl.multiple_of(7 * half * LANES + at, LANES)
        src = meas_ref.at[0, :, :, pl.ds(start, PIECE)]
        dst = meas_raw.at[1, :, :, lanes]
        return remote(src, dst, meas_send.at[c], meas_recv.at[c], (r, pair))

    def meas_wait(c):
        lanes = pl.ds(pl.multiple_of(flip(c, 3) * PIECE, LANES), PIECE)
        dst = meas_raw.at[1, :, :, lanes]
        remote(dst, dst, meas_send.at[c], meas_recv.at[c], (r, pair)).wait_recv()


    def relay_copy(i, k):
        to = (r, 4 * zh + lax.rem(x + k, 4))
        margin = (near, far)[i].at[8]
        return remote(margin, margin, relay_send.at[i, k - 1], relay_recv.at[i], to)

    def margin_wait(i):
        @pl.when(jnp.logical_not(relay))
        def _():
            relay_copy(i, 1).wait_recv()

    freq_copy.start()

    @pl.when(owner)
    def _():
        edge_each(True, lambda copy: copy.start())

    for k in range(1, 4):
        slab_copy(0, k).start()

    @pl.when(jnp.logical_not(owner))
    def _():
        for c in range(3):
            meas_copy(c).start()

    for k in range(1, 4):
        slab_copy(1, k).start()

    def halo_copy(s, t, c, down):
        lo = 0 if down else 2 * ROWS
        i = 0 if down else 1
        u0, u1 = SLAB_PARTS[c] if s == 0 else PARTS[c]
        ref = near if s == 0 else halo.at[s - 1, t]
        return remote(
            ref.at[u0:u1, ROWS : 2 * ROWS, :],
            ref.at[u0:u1, lo : lo + ROWS, :],
            halo_send.at[s, t, c, i],
            halo_recv.at[s, t, c, i],
            (dn if down else up, a),
        )

    def halo_each(s, t, c, sending, act):
        @pl.when(has_dn if sending else has_up)
        def _():
            act(halo_copy(s, t, c, True))

        @pl.when(has_up if sending else has_dn)
        def _():
            act(halo_copy(s, t, c, False))

    def halo_start(s, t, c):
        halo_each(s, t, c, True, lambda copy: copy.start())

    def halo_wait(s, t, c):
        halo_each(s, t, c, False, lambda copy: copy.wait_recv())

    def halo_done(s, t, c):
        halo_each(s, t, c, True, lambda copy: copy.wait_send())

    def columns(ref, w, u0, u1):
        rows = ref.shape[1]
        acc = None
        for j in range(3):
            lhs = ref[u0 + j : u1 + j].reshape((u1 - u0) * rows, 2 * LANES)
            term = jnp.dot(lhs, w[j], preferred_element_type=F32)
            acc = term if acc is None else acc + term
        return acc.astype(BF16).reshape(u1 - u0, rows, 2 * LANES)

    def own(s, t, u0, u1, value):
        halo[s - 1, t, u0:u1, ROWS : 2 * ROWS, :] = value

    def enter(t):
        at = 0
        for c, (u0, u1) in enumerate(PARTS):
            if t == 0:
                if c < 2:
                    halo_wait(0, 0, c)
                else:
                    margin_wait(0)
            ahead = min(u1 + 1, UNITS)
            for u in range(at, ahead):
                re, im = times(*parts(near[u]), *parts(inc[t, u]))
                entry[t, u + 1] = join(re, im).astype(BF16)
            at = ahead
            first[t, u0:u1] = columns(entry.at[t], wf, u0, u1)

    def second(t):
        for u in range(UNITS):
            re, im = row_correlate(rf, first[t, u])
            value = join(re, im).astype(BF16)
            inner[t, u] = value
            re, im = times(*parts(far[u]), *parts(value))
            field[t, u + 1] = join(re, im).astype(BF16)
        for c, (u0, u1) in enumerate(PARTS):
            own(1, t, u0, u1, columns(field.at[t], wf, u0, u1))
            halo_start(1, t, c)

    def compare(t, c):
        halo_wait(1, t, c)
        lanes = pl.ds(pl.multiple_of(flip(c, 3) * PIECE, LANES), PIECE)
        meas_wide[...] = meas_raw[t, :, :, lanes].astype(F32)
        for k in range(3):
            u = 3 * c + k
            re, im = row_correlate(rf, halo[0, t, u])
            value = join(re, im).astype(BF16)
            lanes = pl.ds(pl.multiple_of(flip(k, 3) * LANES, LANES), LANES)
            target = join(meas_wide[:, 0, lanes], meas_wide[:, 1, lanes])
            halo[1, t, u, ROWS : 2 * ROWS, :] = (value.astype(F32) - target).astype(BF16)
        halo_start(2, t, c)

    def back(s, t, c):
        halo_wait(s, t, c)
        for u in range(*PARTS[c]):
            re, im = row_correlate(ra, halo[s - 1, t, u])
            field[t, u + 1] = join(re, im).astype(BF16)

    def add(t, total, pack, u0, u1, re, im):
        grad = join(re, im)
        if t == 0:
            total[u0:u1] = grad
        else:
            grad = grad + total[u0:u1]
            total[u0:u1] = grad
            pack[u0:u1] = grad.astype(BF16)

    def back_far(t):
        def piece(c):
            u0, u1 = PARTS[c]
            br, bi = parts(columns(field.at[t], wa, u0, u1))
            re, im = conj_times(*parts(far[u0:u1]), br, bi)
            own(3, t, u0, u1, join(re, im).astype(BF16))
            halo_start(3, t, c)
            re, im = conj_times(*parts(inner[t, u0:u1]), br, bi)
            add(t, sum_far, pack_far, u0, u1, re, im)

        back(2, t, 0)
        back(2, t, 1)
        piece(0)
        back(2, t, 2)
        piece(1)
        piece(2)

    def back_near(t):
        def piece(c):
            u0, u1 = PARTS[c]
            br, bi = parts(columns(field.at[t], wa, u0, u1))
            re, im = conj_times(*parts(inc[t, u0:u1, ROWS : 2 * ROWS]), br, bi)
            add(t, sum_near, pack_near, u0, u1, re, im)

        back(3, t, 0)
        back(3, t, 1)
        piece(0)
        back(3, t, 2)
        piece(1)
        piece(2)

    grads = ((pack_near, got_near, sum_near), (pack_far, got_far, sum_far))

    def grad_copy(i, k):
        to = lax.rem(x + k, 4)
        src = grads[i][0].at[pl.ds(first_of(to), 2)]
        dst = grads[i][1].at[k - 1]
        return remote(src, dst, grad_send.at[i, k - 1], grad_recv.at[i, k - 1], (r, 4 * zh + to))

    def finish(i):
        _, got, total = grads[i]
        for k in range(1, 4):
            grad_copy(i, k).wait_recv()
        for j in range(2):
            at = flip(j, 2)
            value = total[mine + at]
            for k in range(3):
                value = value + got[k, at].astype(F32)
            result[i, :, 0, j * LANES : (j + 1) * LANES] = value[:, :LANES]
            result[i, :, 1, j * LANES : (j + 1) * LANES] = value[:, LANES:]

    waves(0, freq)
    for t in range(2):
        entry[t, 0] = jnp.zeros((3 * ROWS, 2 * LANES), BF16)
        entry[t, UNITS + 1] = jnp.zeros((3 * ROWS, 2 * LANES), BF16)
        field[t, 0] = jnp.zeros((ROWS, 2 * LANES), BF16)
        field[t, UNITS + 1] = jnp.zeros((ROWS, 2 * LANES), BF16)

    for k in range(1, 4):
        slab_wait(0, k)
    halo_start(0, 0, 0)
    halo_start(0, 0, 1)

    @pl.when(owner)
    def _():
        for c in range(3):
            meas_copy(c).start()

    @pl.when(relay)
    def _():
        edge_each(False, lambda copy: copy.wait_recv())
        for i in range(2):
            for k in range(1, 4):
                relay_copy(i, k).start()

    for k in range(1, 4):
        slab_wait(1, k)
    enter(0)
    margin_wait(1)
    second(0)
    freq_copy.wait_recv()
    waves(1, other_freq)
    enter(1)
    second(1)
    meas_load.wait()
    for c in range(3):
        compare(0, c)
    for c in range(3):
        meas_wait(c)
        compare(1, c)
    back_far(0)
    back_far(1)
    for k in range(1, 4):
        grad_copy(1, k).start()
    back_near(0)
    back_near(1)
    for k in range(1, 4):
        grad_copy(0, k).start()
    stores = [pltpu.make_async_copy(result.at[i], out.at[i], load_sem.at[2 + i]) for i in range(2)]
    finish(1)
    stores[1].start()
    finish(0)
    stores[0].start()

    for i in range(2):
        for k in range(1, 4):
            slab_copy(i, k).wait_send()
            grad_copy(i, k).wait_send()

        @pl.when(owner)
        def _():
            if i == 0:
                edge_each(True, lambda copy: copy.wait_send())

        @pl.when(relay)
        def _():
            for k in range(1, 4):
                relay_copy(i, k).wait_send()

    freq_copy.wait_send()
    for c in range(3):
        meas_copy(c).wait_send()
    for store in stores:
        store.wait()
    halo_done(0, 0, 0)
    halo_done(0, 0, 1)
    for s in range(1, 4):
        for t in range(2):
            for c in range(3):
                halo_done(s, t, c)


def local(rows_n, measured, slices, kernel_taps, angle_freq, chosen):
    length = measured.shape[3]
    unit = (ROWS, 2 * LANES)
    wide = (3 * ROWS, 2 * LANES)
    vmem = pl.BlockSpec(memory_space=pltpu.VMEM)
    smem = pl.BlockSpec(memory_space=pltpu.SMEM)
    hbm = pl.BlockSpec(memory_space=pltpu.HBM)
    dma = pltpu.SemaphoreType.DMA
    grads = pl.pallas_call(
        functools.partial(kernel, rows_n, length),
        out_shape=jax.ShapeDtypeStruct((2, ROWS, 2, 2 * LANES), F32),
        in_specs=[smem, smem, vmem, hbm, hbm],
        out_specs=pl.BlockSpec(memory_space=pl.ANY),
        scratch_shapes=[
            pltpu.VMEM((2, ROWS, 2, 2 * LANES), BF16),
            pltpu.VMEM((ROWS, 2, 2 * LANES), F32),
            pltpu.VMEM((2, ROWS, 2, UNITS * LANES), BF16),
            pltpu.VMEM((ROWS, 2, PIECE), F32),
            pltpu.VMEM((UNITS,) + wide, BF16),
            pltpu.VMEM((UNITS,) + unit, BF16),
            pltpu.VMEM((2, LANES), F32),
            pltpu.VMEM((2, LANES), F32),
            pltpu.VMEM((8, 4 * LANES), F32),
            pltpu.VMEM((3, 2 * LANES, 2 * LANES), BF16),
            pltpu.VMEM((3, 2 * LANES, 2 * LANES), BF16),
            pltpu.VMEM((2 * ROWS, LANES), BF16),
            pltpu.VMEM((2 * ROWS, LANES), BF16),
            pltpu.VMEM((2, UNITS) + wide, F32),
            pltpu.VMEM((2, UNITS) + unit, BF16),
            pltpu.VMEM((2, UNITS + 2) + wide, BF16),
            pltpu.VMEM((2, UNITS) + wide, BF16),
            pltpu.VMEM((2, UNITS + 2) + unit, BF16),
            pltpu.VMEM((3, 2, UNITS) + wide, BF16),
            pltpu.VMEM((UNITS,) + unit, F32),
            pltpu.VMEM((UNITS,) + unit, F32),
            pltpu.VMEM((UNITS,) + unit, BF16),
            pltpu.VMEM((UNITS,) + unit, BF16),
            pltpu.VMEM((3, 2) + unit, BF16),
            pltpu.VMEM((3, 2) + unit, BF16),
            pltpu.VMEM((2, ROWS, 2, 2 * LANES), F32),
            dma((4,)),
            dma((2, 3)),
            dma((2, 3)),
            dma((2, 3)),
            dma((2, 3)),
            dma((2, 3)),
            dma((2,)),
            dma,
            dma,
            dma((3,)),
            dma((3,)),
            dma((4, 2, 3, 2)),
            dma((4, 2, 3, 2)),
            dma((2, 3)),
            dma((2, 3)),
        ],
        compiler_params=pltpu.CompilerParams(
            collective_id=0, has_side_effects=True, vmem_limit_bytes=24 * 2**20
        ),
    )(
        chosen,
        pltpu.with_memory_space_constraint(angle_freq.T, pltpu.HBM),
        pltpu.with_memory_space_constraint(kernel_taps, pltpu.HBM),
        pltpu.with_memory_space_constraint(slices, pltpu.HBM),
        pltpu.with_memory_space_constraint(measured, pltpu.HBM),
    )
    return grads[0], grads[1]


def solution(mesh):
    return jax.shard_map(
        functools.partial(local, mesh.shape["rows"]),
        mesh=mesh,
        in_specs=(P("ang", "rows", None, None), P(None, "rows", None, "ang"), P(), P(), P("ang")),
        out_specs=(P("rows", None, "ang"), P("rows", None, "ang")),
        check_vma=False,
    )
```

```python
import functools
import math

import jax
import jax.numpy as jnp
from jax import lax
from jax.experimental import pallas as pl
from jax.experimental.pallas import tpu as pltpu
from jax.sharding import PartitionSpec as P

MESH = pl.DeviceIdType.MESH
F32 = jnp.float32
BF16 = jnp.bfloat16
ROWS = 32
LANES = 128
UNITS = 9
REACH = 32
TAPS = 65


def build_taps(zh, taps_ref, line, wf, wa, rf, ra):
    line[...] = jnp.zeros_like(line)
    line[0:2, 0:TAPS] = taps_ref[...].astype(F32)
    gr = line[0:1, :]
    gi = line[1:2, :]

    def column(vec, j):
        wide = jnp.broadcast_to(vec, (LANES, 4 * LANES))
        shift = (LANES * (j - 1) - REACH) % (4 * LANES)
        return pltpu.roll(wide, shift, 1, stride=1, stride_axis=0)[:, :LANES]

    for j in range(3):
        re = column(gr, j)
        im = column(gi, j)
        ja = j + zh * (2 - 2 * j)
        jf = 2 - ja
        wa[ja, 0:LANES, 0:LANES] = re.astype(BF16)
        wa[ja, 0:LANES, LANES:] = (-im).astype(BF16)
        wa[ja, LANES:, 0:LANES] = im.astype(BF16)
        wa[ja, LANES:, LANES:] = re.astype(BF16)
        ret = re.T
        imt = im.T
        wf[jf, 0:LANES, 0:LANES] = ret.astype(BF16)
        wf[jf, 0:LANES, LANES:] = imt.astype(BF16)
        wf[jf, LANES:, 0:LANES] = (-imt).astype(BF16)
        wf[jf, LANES:, LANES:] = ret.astype(BF16)

    def row(vec, sign):
        narrow = vec[:, :LANES]
        ahead = pltpu.roll(jnp.broadcast_to(narrow, (ROWS, LANES)), 0, 1, stride=1, stride_axis=0)
        back = pltpu.roll(
            jnp.broadcast_to(narrow, (LANES, LANES)), LANES - 2 * REACH, 1, stride=1, stride_axis=0
        )
        return ahead, sign * back.T[0:ROWS, :]

    fr, br = row(gr, 1.0)
    fi, bi = row(gi, -1.0)
    rf[0:ROWS, :] = fr.astype(BF16)
    rf[ROWS:, :] = fi.astype(BF16)
    ra[0:ROWS, :] = br.astype(BF16)
    ra[ROWS:, :] = bi.astype(BF16)


def row_correlate(taps, window):
    both = jnp.dot(taps[:, 0 : 3 * ROWS], window, preferred_element_type=F32)
    re = both[:ROWS, :LANES] - both[ROWS:, LANES:]
    im = both[:ROWS, LANES:] + both[ROWS:, :LANES]
    return re, im


def times(ar, ai, br, bi):
    return ar * br - ai * bi, ar * bi + ai * br


def conj_times(ar, ai, br, bi):
    return ar * br + ai * bi, ar * bi - ai * br


def join(re, im):
    return jnp.concatenate([re, im], axis=-1)


def parts(value):
    value = value.astype(F32)
    return value[..., :LANES], value[..., LANES:]


SLAB_PARTS = ((0, 4), (4, 8))
PARTS = ((0, 3), (3, 6), (6, 9))
PIECE = 3 * LANES


def kernel(
    rows_n,
    length,
    chosen_ref,
    table_ref,
    taps_ref,
    slices_ref,
    meas_ref,
    out,
    slab_raw,
    slab_wide,
    meas_raw,
    meas_wide,
    near,
    far,
    freq,
    other_freq,
    line,
    wf,
    wa,
    rf,
    ra,
    inc,
    inner,
    entry,
    first,
    field,
    halo,
    sum_near,
    sum_far,
    pack_near,
    pack_far,
    got_near,
    got_far,
    result,
    load_sem,
    slab_send,
    slab_recv,
    edge_send,
    edge_recv,
    relay_send,
    relay_recv,
    freq_send,
    freq_recv,
    meas_send,
    meas_recv,
    halo_send,
    halo_recv,
    grad_send,
    grad_recv,
):
    r = lax.axis_index("rows")
    a = lax.axis_index("ang")
    zh = a // 4
    x = lax.rem(a, 4)
    has_up = r > 0
    has_dn = r < rows_n - 1
    up = lax.rem(r + rows_n - 1, rows_n)
    dn = lax.rem(r + 1, rows_n)
    pair = lax.rem(a + 4, 8)

    def first_of(other_x):
        return 2 * other_x + zh * (6 - 4 * other_x)

    mine = first_of(x)

    def flip(i, n):
        return i + zh * (n - 1 - 2 * i)

    barrier = pltpu.get_barrier_semaphore()
    pl.semaphore_signal(barrier, inc=1, device_id=(r, pair), device_id_type=MESH)
    for k in range(1, 4):
        to = (r, 4 * zh + lax.rem(x + k, 4))
        pl.semaphore_signal(barrier, inc=1, device_id=to, device_id_type=MESH)

    owner = mine == 6
    relay = mine == 0
    end = jnp.logical_or(owner, relay)
    for has, row in ((has_up, up), (has_dn, dn)):

        @pl.when(has)
        def _():
            pl.semaphore_signal(barrier, inc=1, device_id=(row, a), device_id_type=MESH)

        @pl.when(jnp.logical_and(has, end))
        def _():
            pl.semaphore_signal(barrier, inc=1, device_id=(row, pair), device_id_type=MESH)

    def meas_from(half):
        return meas_ref.at[0, :, :, pl.ds(pl.multiple_of(7 * half * LANES, LANES), UNITS * LANES)]

    slab_load = pltpu.make_async_copy(slices_ref, slab_raw, load_sem.at[0])
    slab_load.start()
    meas_load = pltpu.make_async_copy(meas_from(zh), meas_raw.at[0], load_sem.at[1])
    meas_load.start()

    fy = table_ref[0, chosen_ref[0]]
    fx = table_ref[1, chosen_ref[0]]
    freq[0:1, :] = jnp.full((1, LANES), fy, F32)
    freq[1:2, :] = jnp.full((1, LANES), fx, F32)

    slab_load.wait()

    def slab(i, unit, n):
        if i == 0:
            return near.at[pl.ds(unit, n), ROWS : 2 * ROWS, :]
        return far.at[pl.ds(unit, n)]

    for i in range(2):
        slab_wide[...] = slab_raw[i].astype(F32)
        for k in range(2):
            lanes = slice(k * LANES, (k + 1) * LANES)
            unit = join(slab_wide[:, 0, lanes], slab_wide[:, 1, lanes])
            slab(i, mine + flip(k, 2), 1)[...] = unit.astype(BF16)[None]

    build_taps(zh, taps_ref, line, wf, wa, rf, ra)

    def waves(t, ref):
        vy = ref[0:1, :]
        vx = ref[1:2, :]
        unit = lax.broadcasted_iota(jnp.int32, (16, LANES), 0)
        wide = lax.broadcasted_iota(jnp.int32, (3 * ROWS, LANES), 0)
        pos_r = ((r - 1) * ROWS + wide).astype(F32)
        pos_c = (flip(unit, 16) * LANES + lax.broadcasted_iota(jnp.int32, (16, LANES), 1)).astype(F32)
        turn_r = (vy * pos_r) * (1.0 / length)
        turn_c = (vx * pos_c) * (1.0 / length)
        ang_r = (2.0 * math.pi) * (turn_r - jnp.floor(turn_r + 0.5))
        ang_c = (2.0 * math.pi) * (turn_c - jnp.floor(turn_c + 0.5))
        cr, sr = jnp.cos(ang_r), jnp.sin(ang_r)
        cc, sc = jnp.cos(ang_c), jnp.sin(ang_c)
        for u in range(UNITS):
            re, im = times(cr, sr, cc[u : u + 1, :], sc[u : u + 1, :])
            inc[t, u, :, 0:LANES] = re
            inc[t, u, :, LANES:] = im

    @pl.when(jnp.logical_not(has_up))
    def _():
        near[:, 0:ROWS, :] = jnp.zeros((UNITS, ROWS, 2 * LANES), BF16)
        halo[:, :, :, 0:ROWS, :] = jnp.zeros((3, 2, UNITS, ROWS, 2 * LANES), BF16)

    @pl.when(jnp.logical_not(has_dn))
    def _():
        near[:, 2 * ROWS :, :] = jnp.zeros((UNITS, ROWS, 2 * LANES), BF16)
        halo[:, :, :, 2 * ROWS :, :] = jnp.zeros((3, 2, UNITS, ROWS, 2 * LANES), BF16)

    beside = has_up.astype(jnp.int32) + has_dn.astype(jnp.int32)
    pl.semaphore_wait(barrier, 4 + beside * (1 + end.astype(jnp.int32)))

    def remote(src, dst, send_sem, recv_sem, to):
        return pltpu.make_async_remote_copy(
            src_ref=src,
            dst_ref=dst,
            send_sem=send_sem,
            recv_sem=recv_sem,
            device_id=to,
            device_id_type=MESH,
        )

    def slab_copy(i, k):
        block = slab(i, mine, 2)
        to = (r, 4 * zh + lax.rem(x + k, 4))
        return remote(block, block, slab_send.at[i, k - 1], slab_recv.at[i, k - 1], to)

    def slab_wait(i, k):
        block = slab(i, first_of(lax.rem(x + 4 - k, 4)), 2)
        remote(block, block, slab_send.at[i, k - 1], slab_recv.at[i, k - 1], (r, pair)).wait_recv()

    def edge_copy(i, d):
        lo = ROWS - ROWS * d
        dst = near.at[8:9, lo : lo + ROWS, :] if i == 0 else slab(1, 8, 1)
        row = (up, r, dn)[d + 1]
        sems = edge_send.at[i, d + 1], edge_recv.at[i, d + 1]
        return remote(slab(i, 7, 1), dst, *sems, (row, pair))

    def edge_each(sending, act):
        act(edge_copy(0, 0))
        act(edge_copy(1, 0))
        for d in (-1, 1):
            @pl.when(has_up if (d < 0) == sending else has_dn)
            def _():
                act(edge_copy(0, d))

    freq_copy = remote(freq, other_freq, freq_send, freq_recv, (r, pair))
    def meas_copy(c):
        half = 1 - zh
        at = (c + half * (2 - 2 * c)) * PIECE
        lanes = pl.ds(pl.multiple_of(at, LANES), PIECE)
        start = pl.multiple_of(7 * half * LANES + at, LANES)
        src = meas_ref.at[0, :, :, pl.ds(start, PIECE)]
        dst = meas_raw.at[1, :, :, lanes]
        return remote(src, dst, meas_send.at[c], meas_recv.at[c], (r, pair))

    def meas_wait(c):
        lanes = pl.ds(pl.multiple_of(flip(c, 3) * PIECE, LANES), PIECE)
        dst = meas_raw.at[1, :, :, lanes]
        remote(dst, dst, meas_send.at[c], meas_recv.at[c], (r, pair)).wait_recv()


    def relay_copy(i, k):
        to = (r, 4 * zh + lax.rem(x + k, 4))
        margin = (near, far)[i].at[8]
        return remote(margin, margin, relay_send.at[i, k - 1], relay_recv.at[i], to)

    def margin_wait(i):
        @pl.when(jnp.logical_not(relay))
        def _():
            relay_copy(i, 1).wait_recv()

    freq_copy.start()

    @pl.when(owner)
    def _():
        edge_each(True, lambda copy: copy.start())

    for k in range(1, 4):
        slab_copy(0, k).start()

    @pl.when(jnp.logical_not(owner))
    def _():
        for c in range(3):
            meas_copy(c).start()

    for k in range(1, 4):
        slab_copy(1, k).start()

    def halo_copy(s, t, c, down):
        lo = 0 if down else 2 * ROWS
        i = 0 if down else 1
        u0, u1 = SLAB_PARTS[c] if s == 0 else PARTS[c]
        ref = near if s == 0 else halo.at[s - 1, t]
        return remote(
            ref.at[u0:u1, ROWS : 2 * ROWS, :],
            ref.at[u0:u1, lo : lo + ROWS, :],
            halo_send.at[s, t, c, i],
            halo_recv.at[s, t, c, i],
            (dn if down else up, a),
        )

    def halo_each(s, t, c, sending, act):
        @pl.when(has_dn if sending else has_up)
        def _():
            act(halo_copy(s, t, c, True))

        @pl.when(has_up if sending else has_dn)
        def _():
            act(halo_copy(s, t, c, False))

    def halo_start(s, t, c):
        halo_each(s, t, c, True, lambda copy: copy.start())

    def halo_wait(s, t, c):
        halo_each(s, t, c, False, lambda copy: copy.wait_recv())

    def halo_done(s, t, c):
        halo_each(s, t, c, True, lambda copy: copy.wait_send())

    def columns(ref, w, u0, u1):
        rows = ref.shape[1]
        acc = None
        for j in range(3):
            lhs = ref[u0 + j : u1 + j].reshape((u1 - u0) * rows, 2 * LANES)
            term = jnp.dot(lhs, w[j], preferred_element_type=F32)
            acc = term if acc is None else acc + term
        return acc.astype(BF16).reshape(u1 - u0, rows, 2 * LANES)

    def own(s, t, u0, u1, value):
        halo[s - 1, t, u0:u1, ROWS : 2 * ROWS, :] = value

    def enter(t):
        at = 0
        for c, (u0, u1) in enumerate(PARTS):
            if t == 0:
                if c < 2:
                    halo_wait(0, 0, c)
                else:
                    margin_wait(0)
            ahead = min(u1 + 1, UNITS)
            for u in range(at, ahead):
                re, im = times(*parts(near[u]), *parts(inc[t, u]))
                entry[t, u + 1] = join(re, im).astype(BF16)
            at = ahead
            first[t, u0:u1] = columns(entry.at[t], wf, u0, u1)

    def second(t):
        at = 0
        for c, (u0, u1) in enumerate(PARTS):
            ahead = min(u1 + 1, UNITS)
            for u in range(at, ahead):
                re, im = row_correlate(rf, first[t, u])
                value = join(re, im).astype(BF16)
                inner[t, u] = value
                re, im = times(*parts(far[u]), *parts(value))
                field[t, u + 1] = join(re, im).astype(BF16)
            at = ahead
            own(1, t, u0, u1, columns(field.at[t], wf, u0, u1))
            halo_start(1, t, c)

    def compare(t, c):
        halo_wait(1, t, c)
        lanes = pl.ds(pl.multiple_of(flip(c, 3) * PIECE, LANES), PIECE)
        meas_wide[...] = meas_raw[t, :, :, lanes].astype(F32)
        for k in range(3):
            u = 3 * c + k
            re, im = row_correlate(rf, halo[0, t, u])
            value = join(re, im).astype(BF16)
            lanes = pl.ds(pl.multiple_of(flip(k, 3) * LANES, LANES), LANES)
            target = join(meas_wide[:, 0, lanes], meas_wide[:, 1, lanes])
            halo[1, t, u, ROWS : 2 * ROWS, :] = (value.astype(F32) - target).astype(BF16)
        halo_start(2, t, c)

    def back(s, t, c):
        halo_wait(s, t, c)
        for u in range(*PARTS[c]):
            re, im = row_correlate(ra, halo[s - 1, t, u])
            field[t, u + 1] = join(re, im).astype(BF16)

    def add(t, total, pack, u0, u1, re, im):
        grad = join(re, im)
        if t == 0:
            total[u0:u1] = grad
        else:
            grad = grad + total[u0:u1]
            total[u0:u1] = grad
            pack[u0:u1] = grad.astype(BF16)

    def back_far(t):
        def piece(c):
            u0, u1 = PARTS[c]
            br, bi = parts(columns(field.at[t], wa, u0, u1))
            re, im = conj_times(*parts(far[u0:u1]), br, bi)
            own(3, t, u0, u1, join(re, im).astype(BF16))
            halo_start(3, t, c)
            re, im = conj_times(*parts(inner[t, u0:u1]), br, bi)
            add(t, sum_far, pack_far, u0, u1, re, im)

        back(2, t, 0)
        back(2, t, 1)
        piece(0)
        back(2, t, 2)
        piece(1)
        piece(2)

    def back_near(t):
        def piece(c):
            u0, u1 = PARTS[c]
            br, bi = parts(columns(field.at[t], wa, u0, u1))
            re, im = conj_times(*parts(inc[t, u0:u1, ROWS : 2 * ROWS]), br, bi)
            add(t, sum_near, pack_near, u0, u1, re, im)

        back(3, t, 0)
        back(3, t, 1)
        piece(0)
        back(3, t, 2)
        piece(1)
        piece(2)

    grads = ((pack_near, got_near, sum_near), (pack_far, got_far, sum_far))

    def grad_copy(i, k):
        to = lax.rem(x + k, 4)
        src = grads[i][0].at[pl.ds(first_of(to), 2)]
        dst = grads[i][1].at[k - 1]
        return remote(src, dst, grad_send.at[i, k - 1], grad_recv.at[i, k - 1], (r, 4 * zh + to))

    def finish(i):
        _, got, total = grads[i]
        for k in range(1, 4):
            grad_copy(i, k).wait_recv()
        for j in range(2):
            at = flip(j, 2)
            value = total[mine + at]
            for k in range(3):
                value = value + got[k, at].astype(F32)
            result[i, :, 0, j * LANES : (j + 1) * LANES] = value[:, :LANES]
            result[i, :, 1, j * LANES : (j + 1) * LANES] = value[:, LANES:]

    waves(0, freq)
    for t in range(2):
        entry[t, 0] = jnp.zeros((3 * ROWS, 2 * LANES), BF16)
        entry[t, UNITS + 1] = jnp.zeros((3 * ROWS, 2 * LANES), BF16)
        field[t, 0] = jnp.zeros((ROWS, 2 * LANES), BF16)
        field[t, UNITS + 1] = jnp.zeros((ROWS, 2 * LANES), BF16)

    for k in range(1, 4):
        slab_wait(0, k)
    halo_start(0, 0, 0)
    halo_start(0, 0, 1)

    @pl.when(owner)
    def _():
        for c in range(3):
            meas_copy(c).start()

    @pl.when(relay)
    def _():
        edge_each(False, lambda copy: copy.wait_recv())
        for i in range(2):
            for k in range(1, 4):
                relay_copy(i, k).start()

    for k in range(1, 4):
        slab_wait(1, k)
    enter(0)
    margin_wait(1)
    second(0)
    freq_copy.wait_recv()
    waves(1, other_freq)
    enter(1)
    second(1)
    meas_load.wait()
    for c in range(3):
        compare(0, c)
    for c in range(3):
        meas_wait(c)
        compare(1, c)
    back_far(0)
    back_far(1)
    for k in range(1, 4):
        grad_copy(1, k).start()
    back_near(0)
    back_near(1)
    for k in range(1, 4):
        grad_copy(0, k).start()
    stores = [pltpu.make_async_copy(result.at[i], out.at[i], load_sem.at[2 + i]) for i in range(2)]
    finish(1)
    stores[1].start()
    finish(0)
    stores[0].start()

    for i in range(2):
        for k in range(1, 4):
            slab_copy(i, k).wait_send()
            grad_copy(i, k).wait_send()

        @pl.when(owner)
        def _():
            if i == 0:
                edge_each(True, lambda copy: copy.wait_send())

        @pl.when(relay)
        def _():
            for k in range(1, 4):
                relay_copy(i, k).wait_send()

    freq_copy.wait_send()
    for c in range(3):
        meas_copy(c).wait_send()
    for store in stores:
        store.wait()
    halo_done(0, 0, 0)
    halo_done(0, 0, 1)
    for s in range(1, 4):
        for t in range(2):
            for c in range(3):
                halo_done(s, t, c)


def local(rows_n, measured, slices, kernel_taps, angle_freq, chosen):
    length = measured.shape[3]
    unit = (ROWS, 2 * LANES)
    wide = (3 * ROWS, 2 * LANES)
    vmem = pl.BlockSpec(memory_space=pltpu.VMEM)
    smem = pl.BlockSpec(memory_space=pltpu.SMEM)
    hbm = pl.BlockSpec(memory_space=pltpu.HBM)
    dma = pltpu.SemaphoreType.DMA
    grads = pl.pallas_call(
        functools.partial(kernel, rows_n, length),
        out_shape=jax.ShapeDtypeStruct((2, ROWS, 2, 2 * LANES), F32),
        in_specs=[smem, smem, vmem, hbm, hbm],
        out_specs=pl.BlockSpec(memory_space=pl.ANY),
        scratch_shapes=[
            pltpu.VMEM((2, ROWS, 2, 2 * LANES), BF16),
            pltpu.VMEM((ROWS, 2, 2 * LANES), F32),
            pltpu.VMEM((2, ROWS, 2, UNITS * LANES), BF16),
            pltpu.VMEM((ROWS, 2, PIECE), F32),
            pltpu.VMEM((UNITS,) + wide, BF16),
            pltpu.VMEM((UNITS,) + unit, BF16),
            pltpu.VMEM((2, LANES), F32),
            pltpu.VMEM((2, LANES), F32),
            pltpu.VMEM((8, 4 * LANES), F32),
            pltpu.VMEM((3, 2 * LANES, 2 * LANES), BF16),
            pltpu.VMEM((3, 2 * LANES, 2 * LANES), BF16),
            pltpu.VMEM((2 * ROWS, LANES), BF16),
            pltpu.VMEM((2 * ROWS, LANES), BF16),
            pltpu.VMEM((2, UNITS) + wide, F32),
            pltpu.VMEM((2, UNITS) + unit, BF16),
            pltpu.VMEM((2, UNITS + 2) + wide, BF16),
            pltpu.VMEM((2, UNITS) + wide, BF16),
            pltpu.VMEM((2, UNITS + 2) + unit, BF16),
            pltpu.VMEM((3, 2, UNITS) + wide, BF16),
            pltpu.VMEM((UNITS,) + unit, F32),
            pltpu.VMEM((UNITS,) + unit, F32),
            pltpu.VMEM((UNITS,) + unit, BF16),
            pltpu.VMEM((UNITS,) + unit, BF16),
            pltpu.VMEM((3, 2) + unit, BF16),
            pltpu.VMEM((3, 2) + unit, BF16),
            pltpu.VMEM((2, ROWS, 2, 2 * LANES), F32),
            dma((4,)),
            dma((2, 3)),
            dma((2, 3)),
            dma((2, 3)),
            dma((2, 3)),
            dma((2, 3)),
            dma((2,)),
            dma,
            dma,
            dma((3,)),
            dma((3,)),
            dma((4, 2, 3, 2)),
            dma((4, 2, 3, 2)),
            dma((2, 3)),
            dma((2, 3)),
        ],
        compiler_params=pltpu.CompilerParams(
            collective_id=0, has_side_effects=True, vmem_limit_bytes=24 * 2**20
        ),
    )(
        chosen,
        pltpu.with_memory_space_constraint(angle_freq.T, pltpu.HBM),
        pltpu.with_memory_space_constraint(kernel_taps, pltpu.HBM),
        pltpu.with_memory_space_constraint(slices, pltpu.HBM),
        pltpu.with_memory_space_constraint(measured, pltpu.HBM),
    )
    return grads[0], grads[1]


def solution(mesh):
    return jax.shard_map(
        functools.partial(local, mesh.shape["rows"]),
        mesh=mesh,
        in_specs=(P("ang", "rows", None, None), P(None, "rows", None, "ang"), P(), P(), P("ang")),
        out_specs=(P("rows", None, "ang"), P("rows", None, "ang")),
        check_vma=False,
    )
```
